256 devices in a mesh: block: 64 (over x_lo, z, y), piece: 4 (over x_hi, core).
Axes of the slice: x: 4 (x_hi: 2, x_lo: 2; x = x_hi * 2 + x_lo), y: 4, z: 8, core: 2. Of those that a mesh axis runs over, the one named last changes fastest.
Arguments:
- normalized_feature_vectors: float32 [32768, 1152], P(('block', 'piece')), may hold values from -1 to 1, as said below
- view_group_ids: int32 [32768], P(('block', 'piece')), may hold values from 0 to 16383, as said below
- processor_active_segments: int32 [64, 4], P('block', 'piece'), may hold values from 1 to 2, as said below
- segment_couple_multiplicity: int32 [64, 64], replicated, may hold values from 1 to 5, as said below
- logit_scaling: float32 [1], replicated, may hold values from 4 to 16
- logit_offset: float32 [1], replicated, may hold values from -3 to -0.5
Outputs:
- gradient: float32 [32768, 1152], P(('block', 'piece'))
The draws below stay inside these ranges and needn't reach their ends.
Inputs may be any that keep to these rules, and one draw needn't show every extreme that they name: `normalized_feature_vectors`: every row has unit length; rows of one view group lie near a common direction. `view_group_ids`: the view group of each row; a group's rows may stand on any devices. A device's first processor_active_segments * 64 rows are live and the rest are padding; some device has all 2 live in every draw. `segment_couple_multiplicity`: symmetric.
All inputs are finite; a program needn't handle non-finite values.
Results may differ from the reference program's by a relative error of at most 0.0031.
Values may be sent and summed in bfloat16 or wider, within the bound.
A program may use at most 128 MiB of HBM per device.

```python
import math
import jax
import jax.numpy as jnp
from jax import lax

D = 1152
TILE = 64
TILES_DEV = 2
BLOCKS = 64
PIECES = 4
NROWS = 32768
GROUPS = 16384
N_BLOCK = 64
N_PIECE = 4


def group_labels(key):
    return jax.random.randint(jax.random.fold_in(key, 7), (NROWS,), 0, GROUPS).astype(jnp.int32)


def draw_view_group_ids(key, part):
    return group_labels(key)


def draw_normalized_feature_vectors(key, part):
    members = group_labels(key)
    cluster_means = jax.random.normal(jax.random.fold_in(key, 8), (GROUPS, D), jnp.float32)
    noise = jax.random.normal(jax.random.fold_in(key, 9), (NROWS, D), jnp.float32)
    raw_rows = cluster_means[members] + 0.8 * noise
    return raw_rows / jnp.sqrt(jnp.sum(raw_rows * raw_rows, axis=1, keepdims=True))


def draw_processor_active_segments(key, part):
    counts = jax.random.randint(jax.random.fold_in(key, 3), (BLOCKS * PIECES,), 1, TILES_DEV + 1)
    chosen = jax.random.randint(jax.random.fold_in(key, 4), (), 0, BLOCKS * PIECES)
    counts = jnp.where(jnp.arange(BLOCKS * PIECES) == chosen, TILES_DEV, counts)
    return counts.reshape(BLOCKS, PIECES).astype(jnp.int32)


def draw_segment_couple_multiplicity(key, part):
    halves = jax.random.randint(jax.random.fold_in(key, 5), (BLOCKS, BLOCKS), 0, 3)
    return (1 + halves + halves.T).astype(jnp.int32)


def setup_inputs(seed: int = 0) -> dict:
    splits = jax.random.split(jax.random.key(seed), 7)
    return {
        "normalized_feature_vectors": draw_normalized_feature_vectors(jax.random.fold_in(splits[6], 71), 0),
        "view_group_ids": draw_view_group_ids(jax.random.fold_in(splits[6], 71), 0),
        "processor_active_segments": draw_processor_active_segments(jax.random.fold_in(splits[6], 71), 0),
        "segment_couple_multiplicity": draw_segment_couple_multiplicity(jax.random.fold_in(splits[6], 71), 0),
        "logit_scaling": jnp.clip(jnp.exp(jax.random.uniform(splits[4], (1,), jnp.float32, math.log(4.0), math.log(16.0))), 4.0, 16.0),
        "logit_offset": jnp.clip(jax.random.uniform(splits[5], (1,), jnp.float32, -3.0, -0.5), -3.0, -0.5),
    }


def reference(normalized_feature_vectors, view_group_ids, processor_active_segments, segment_couple_multiplicity, logit_scaling, logit_offset):
    total_rows, model_width = normalized_feature_vectors.shape
    rows_dev = TILE * TILES_DEV
    block_rows = rows_dev * N_PIECE
    rounded = lax.optimization_barrier(normalized_feature_vectors.astype(jnp.bfloat16)).astype(jnp.float32)
    position = jnp.arange(total_rows, dtype=jnp.int32)
    owner_counts = jnp.repeat(processor_active_segments.reshape(-1), rows_dev, total_repeat_length=total_rows)
    live_rows = (position % rows_dev // TILE < owner_counts).astype(jnp.float32)
    base_scale = math.sqrt(model_width / total_rows) / 8.0
    warmth_multiplier = logit_scaling[0]
    offset = logit_offset[0]

    def one_block(block_index):
        first_row = (block_index * block_rows).astype(jnp.int32)
        block_payload = lax.dynamic_slice_in_dim(rounded, first_row, block_rows, 0)
        block_labels = lax.dynamic_slice_in_dim(view_group_ids, first_row, block_rows, 0)
        block_live = lax.dynamic_slice_in_dim(live_rows, first_row, block_rows, 0)
        scores = jnp.dot(block_payload, rounded.T, precision=lax.Precision.HIGHEST, preferred_element_type=jnp.float32)
        logits = warmth_multiplier * scores + offset
        polarity = jnp.where(block_labels[:, None] == view_group_ids[None, :], 1.0, -1.0).astype(jnp.float32)
        slopes = -polarity * jax.nn.sigmoid(-polarity * logits)
        weight_row = lax.dynamic_index_in_dim(segment_couple_multiplicity, block_index, 0, keepdims=False).astype(jnp.float32)
        column_weights = jnp.repeat(weight_row, block_rows, total_repeat_length=total_rows)
        own_index = first_row + jnp.arange(block_rows, dtype=jnp.int32)
        usable = block_live[:, None] * live_rows[None, :]
        coefficient = base_scale * warmth_multiplier * column_weights[None, :] * slopes * usable
        coefficient = jnp.where(own_index[:, None] == position[None, :], 0.0, coefficient)
        coefficient = lax.optimization_barrier(coefficient.astype(jnp.bfloat16)).astype(jnp.float32)
        return jnp.dot(coefficient, rounded, precision=lax.Precision.HIGHEST, preferred_element_type=jnp.float32)
    result = lax.map(one_block, jnp.arange(N_BLOCK, dtype=jnp.int32))
    return result.reshape(total_rows, model_width)
```

```python
import math

import jax
import jax.numpy as jnp
from jax import lax
from jax.experimental import pallas as pl
from jax.experimental.pallas import tpu as pltpu
from jax.sharding import PartitionSpec as P

MESH = pl.DeviceIdType.MESH
ROWS = 128
HALF = 64
NX, NY, NZ = 4, 4, 8
GATHER, COMPUTE, REDUCE = True, True, True
UNITS_TILE = 2
A_OFFSETS = (0, 1, 3, 2)


def kernel(
    mult_ref, scale_ref, offset_ref, count_ref, x_ref, lab_ref, out_ref,
    jbuf, ibuf, labj, labi, labcol, acc, psend, precv,
    send_a, recv_a, send_b, recv_b, send_c, recv_c, send_z, recv_z, send_p, recv_p,
):
    block = lax.axis_index("block")
    piece = lax.axis_index("piece")
    z = block // NY % NZ
    y = block % NY
    x = piece // 2 * 2 + block // (NY * NZ)
    c = piece % 2

    def device(px, py, pz, pc):
        return (px % 2 * (NY * NZ) + pz * NY + py, px // 2 * 2 + pc)

    def place(a, b, core):
        return (x + a * (1 - core) + b * core) % NX, (y + a * core + b * (1 - core)) % NY

    def slot(a, b, core):
        px, py = place(a, b, core)
        return (px % 2 * NY + py) * 4 + px // 2 * 2 + core

    def plane_device(a, b):
        px, py = place(a, b, c)
        return device(px, py, z, c)

    def z_device(step):
        return device(x, y, (z + step) % NZ, c)

    other_core = device(x, y, z, 1 - c)
    a_up, a_down = plane_device(1, 0), plane_device(3, 0)
    b_up, b_down = plane_device(0, 1), plane_device(0, 3)
    z_up, z_down = z_device(1), z_device(NZ - 1)

    class Unit:
        def __init__(self, rows, labels, index, target, sends, recvs, key, first=0, count=ROWS):
            part = rows.at[index, pl.ds(first, count)]
            self.copies = [
                pltpu.make_async_remote_copy(
                    src_ref=part, dst_ref=part, send_sem=sends.at[(0, *key)], recv_sem=recvs.at[(0, *key)],
                    device_id=target, device_id_type=MESH,
                )
            ]
            if first == 0:
                part = labels.at[index]
                self.copies.append(
                    pltpu.make_async_remote_copy(
                        src_ref=part, dst_ref=part, send_sem=sends.at[(1, *key)], recv_sem=recvs.at[(1, *key)],
                        device_id=target, device_id_type=MESH,
                    )
                )

        def start(self):
            for copy in self.copies:
                copy.start()

        def wait_recv(self):
            for copy in self.copies:
                copy.wait_recv()

        def wait_send(self):
            for copy in self.copies:
                copy.wait_send()

    started = []

    def send(unit):
        unit.start()
        started.append(unit)

    def unit_a(a, target, key, first=0, count=ROWS):
        return Unit(jbuf, labj, slot(a, 0, c), target, send_a, recv_a, (key,), first, count)

    def unit_b(ai, b, target, key, first=0, count=ROWS):
        return Unit(
            jbuf, labj, slot(A_OFFSETS[ai], b, c), target, send_b, recv_b, (ai, key), first, count
        )

    def unit_c(ai, bi, core):
        return Unit(
            jbuf, labj, slot(A_OFFSETS[ai], A_OFFSETS[bi], core), other_core, send_c, recv_c, (ai, bi)
        )

    def unit_z(step, target, key, first=0, count=ROWS):
        return Unit(ibuf, labi, (z + step) % NZ, target, send_z, recv_z, (key,), first, count)

    live_rows = lax.broadcasted_iota(jnp.int32, (ROWS, 1), 0) // HALF < count_ref[0, 0]
    own_slot = slot(0, 0, c)
    own = jnp.where(live_rows, x_ref[...], 0.0).astype(jnp.bfloat16)
    jbuf[own_slot] = own
    ibuf[z] = own
    labj[own_slot] = lab_ref[...]
    labi[z] = lab_ref[...]

    barrier = pltpu.get_barrier_semaphore()
    for neighbour in (a_up, a_down, b_up, b_down, z_up, z_down, other_core):
        pl.semaphore_signal(barrier, inc=1, device_id=neighbour, device_id_type=MESH)
    pl.semaphore_wait(barrier, 7)

    factor = 0.5 * math.sqrt(jbuf.shape[-1] / (ROWS * NX * NY * NZ * 2)) / 8.0 * scale_ref[0]
    half_scale = 0.5 * scale_ref[0]
    half_offset = 0.5 * offset_ref[0]

    def coefficients(scores, same, weight):
        size = factor * weight
        return size * jnp.tanh(half_scale * scores + half_offset) + jnp.where(same, -size, size)

    def weight_of(unit, chunk):
        row_block = x % 2 * (NY * NZ) + unit * NY + y
        column_block = chunk // NY * (NY * NZ) + z * NY + chunk % NY
        return mult_ref[row_block, column_block].astype(jnp.float32)

    if GATHER:
        send(unit_a(0, a_up, 0))
        send(unit_a(0, a_down, 1))
        send(unit_z(0, z_up, 0))
        send(unit_z(0, z_down, 3))
        send(unit_b(0, 0, b_up, 0))
        send(unit_b(0, 0, b_down, 1))
        send(unit_c(0, 0, c))

    acc[...] = jnp.zeros_like(acc)
    if COMPUTE:
        scores = lax.dot_general(own, own, (((1,), (1,)), ((), ())), preferred_element_type=jnp.float32)
        same = jnp.full((ROWS, ROWS), True)
        eye = lax.broadcasted_iota(jnp.int32, (ROWS, ROWS), 0) == lax.broadcasted_iota(
            jnp.int32, (ROWS, ROWS), 1
        )
        diagonal = jnp.where(eye, coefficients(scores, same, weight_of(z, own_slot // 4)), 0.0)
        acc[z] = -jnp.dot(diagonal.astype(jnp.bfloat16), own, preferred_element_type=jnp.float32)

    def forward_b(ai):
        unit_b(ai, 3, b_up, 0).wait_recv()
        send(unit_b(ai, 3, b_up, 2, 0, HALF))
        unit_b(ai, 1, b_down, 1).wait_recv()
        send(unit_b(ai, 1, b_down, 3, HALF, HALF))
        send(unit_c(ai, 2, c))
        send(unit_c(ai, 1, c))

    def far_b(ai):
        unit_b(ai, 2, b_up, 2, 0, HALF).wait_recv()
        unit_b(ai, 2, b_down, 3, HALF, HALF).wait_recv()
        send(unit_c(ai, 3, c))

    def open_b(ai):
        send(unit_b(ai, 0, b_up, 0))
        send(unit_b(ai, 0, b_down, 1))
        send(unit_c(ai, 0, c))

    def forward_z(step):
        unit_z(NZ - step, z_up, step - 1).wait_recv()
        if step < 3:
            send(unit_z(NZ - step, z_up, step))
        else:
            send(unit_z(NZ - step, z_up, 6, 0, HALF))
        unit_z(step, z_down, 3 + step - 1).wait_recv()
        if step < 3:
            send(unit_z(step, z_down, 3 + step))
        else:
            send(unit_z(step, z_down, 7, HALF, HALF))

    if GATHER:
        unit_a(3, a_up, 0).wait_recv()
        send(unit_a(3, a_up, 2, 0, HALF))
        unit_a(1, a_down, 1).wait_recv()
        send(unit_a(1, a_down, 3, HALF, HALF))
        open_b(1)
        open_b(2)
        forward_z(1)
        forward_b(0)
        unit_a(2, a_up, 2, 0, HALF).wait_recv()
        unit_a(2, a_down, 3, HALF, HALF).wait_recv()
        open_b(3)
        forward_z(2)
        far_b(0)
        forward_b(1)
        forward_b(2)
        forward_z(3)
        forward_b(3)
        far_b(1)
        far_b(2)
        far_b(3)
        unit_z(4, z_up, 6, 0, HALF).wait_recv()
        unit_z(4, z_down, 7, HALF, HALF).wait_recv()
        for ai in range(4):
            for bi in range(4):
                unit_c(ai, bi, 1 - c).wait_recv()
        for unit in started:
            unit.wait_send()

    if COMPUTE:
        compute(jbuf, ibuf, labj, labi, labcol, acc, coefficients, weight_of)

    if REDUCE:
        partial_copies = []

        def partial(direction, step, half):
            return pltpu.make_async_remote_copy(
                src_ref=psend.at[direction, step, half],
                dst_ref=precv.at[direction, step, half],
                send_sem=send_p.at[direction, step, half],
                recv_sem=recv_p.at[direction, step, half],
                device_id=z_down if direction else z_up,
                device_id_type=MESH,
            )

        def pass_on(direction, step, half):
            unit = (z + (4 + step if direction else 4 - step)) % NZ
            value = acc[unit, half * HALF : (half + 1) * HALF]
            if step >= 2 or (step == 1 and half == direction):
                partial(direction, step - 1, half).wait_recv()
                value = value + precv[direction, step - 1, half].astype(jnp.float32)
            psend[direction, step, half] = value.astype(jnp.bfloat16)
            copy = partial(direction, step, half)
            copy.start()
            partial_copies.append(copy)

        pass_on(0, 0, 0)
        pass_on(1, 0, 1)
        pass_on(0, 1, 1)
        pass_on(1, 1, 0)
        pass_on(0, 1, 0)
        pass_on(1, 1, 1)
        for step in (2, 3):
            for half in range(2):
                pass_on(0, step, 1 - half)
                pass_on(1, step, half)
        for half in range(2):
            partial(0, 3, half).wait_recv()
            partial(1, 3, half).wait_recv()
            rows = slice(half * HALF, (half + 1) * HALF)
            total = (
                acc[z, rows]
                + precv[0, 3, half].astype(jnp.float32)
                + precv[1, 3, half].astype(jnp.float32)
            )
            out_ref[rows, :] = jnp.where(live_rows[rows], total, 0.0)
        for copy in partial_copies:
            copy.wait_send()
    else:
        out_ref[...] = acc[z]


def compute(jbuf, ibuf, labj, labi, labcol, acc, coefficients, weight_of):
    width = jbuf.shape[-1]

    @pl.loop(0, NZ)
    def _(unit):
        labcol[unit] = jnp.broadcast_to(labi[unit].astype(jnp.float32), (ROWS, ROWS)).T

    @pl.loop(0, 8)
    def _(chunk):
        @pl.loop(0, NZ // UNITS_TILE)
        def _(tile):
            columns = jbuf[pl.ds(chunk * 4, 4)].reshape(4 * ROWS, width)
            rows = ibuf[pl.ds(tile * UNITS_TILE, UNITS_TILE)].reshape(UNITS_TILE * ROWS, width)
            scores = lax.dot_general(
                rows, columns, (((1,), (1,)), ((), ())), preferred_element_type=jnp.float32
            )
            lines = []
            for u in range(UNITS_TILE):
                unit = tile * UNITS_TILE + u
                weight = weight_of(unit, chunk)
                parts = []
                for q in range(4):
                    same = labcol[unit] == labj[chunk * 4 + q].astype(jnp.float32)
                    part = scores[u * ROWS : (u + 1) * ROWS, q * ROWS : (q + 1) * ROWS]
                    parts.append(coefficients(part, same, weight).astype(jnp.bfloat16))
                lines.append(jnp.concatenate(parts, axis=1))
            grads = jnp.dot(
                jnp.concatenate(lines, axis=0), columns, preferred_element_type=jnp.float32
            )
            for u in range(UNITS_TILE):
                acc[tile * UNITS_TILE + u] += grads[u * ROWS : (u + 1) * ROWS]


def shards(rows, labels, counts, multiplicity, scaling, offset):
    width = rows.shape[1]
    smem = pl.BlockSpec(memory_space=pltpu.SMEM)
    vmem = pl.BlockSpec(memory_space=pltpu.VMEM)
    dma = pltpu.SemaphoreType.DMA
    return pl.pallas_call(
        kernel,
        out_shape=jax.ShapeDtypeStruct((ROWS, width), jnp.float32),
        in_specs=[smem, smem, smem, smem, vmem, vmem],
        out_specs=vmem,
        scratch_shapes=[
            pltpu.VMEM((32, ROWS, width), jnp.bfloat16),
            pltpu.VMEM((NZ, ROWS, width), jnp.bfloat16),
            pltpu.VMEM((32, 1, ROWS), jnp.int32),
            pltpu.VMEM((NZ, 1, ROWS), jnp.int32),
            pltpu.VMEM((NZ, ROWS, ROWS), jnp.float32),
            pltpu.VMEM((NZ, ROWS, width), jnp.float32),
            pltpu.VMEM((2, 4, 2, HALF, width), jnp.bfloat16),
            pltpu.VMEM((2, 4, 2, HALF, width), jnp.bfloat16),
            dma((2, 4)), dma((2, 4)), dma((2, 4, 4)), dma((2, 4, 4)), dma((2, 4, 4)), dma((2, 4, 4)),
            dma((2, 8)), dma((2, 8)), dma((2, 4, 2)), dma((2, 4, 2)),
        ],
        compiler_params=pltpu.CompilerParams(
            collective_id=0, has_side_effects=True, vmem_limit_bytes=60 * 1024 * 1024
        ),
    )(multiplicity, scaling, offset, counts, rows, labels.reshape(1, ROWS))


def solution(mesh):
    return jax.shard_map(
        shards,
        mesh=mesh,
        in_specs=(
            P(("block", "piece"), None),
            P(("block", "piece")),
            P("block", "piece"),
            P(),
            P(),
            P(),
        ),
        out_specs=P(("block", "piece"), None),
        check_vma=False,
    )
```

```python
import math

import jax
import jax.numpy as jnp
from jax import lax
from jax.experimental import pallas as pl
from jax.experimental.pallas import tpu as pltpu
from jax.sharding import PartitionSpec as P

MESH = pl.DeviceIdType.MESH
ROWS = 128
HALF = 64
NX, NY, NZ = 4, 4, 8
COMPUTE = True
VMEM_MIB = 60

OFFSETS = (0, 1, 3, 2)
OWN, NEXT, LAST, FAR = range(4)


def z_slot(step):
    return 2 * step - 1 if step > 0 else -2 * step


CHUNKS = (
    ((OWN, OWN), (NEXT, OWN), (LAST, OWN), (OWN, NEXT)),
    ((OWN, LAST), (FAR, OWN), (NEXT, NEXT), (NEXT, LAST)),
    ((OWN, FAR), (LAST, NEXT), (LAST, LAST), (NEXT, FAR)),
    ((LAST, FAR), (FAR, NEXT), (FAR, LAST), (FAR, FAR)),
)
ORDER = {}
for _chunk, _units in enumerate(CHUNKS):
    for _i, _unit in enumerate(_units):
        for _core in range(2):
            ORDER[(*_unit, _core)] = 8 * _chunk + 2 * _i + _core

STEPS = (
    (0, 0), (1, 0), (0, 1), (1, 1), (0, 2), (1, 2), (2, 0), (2, 1),
    (2, 2), (3, 0), (3, 1), (3, 2), (3, 3), (2, 3), (1, 3), (0, 3),
)


def kernel(
    mult_ref, scale_ref, offset_ref, count_ref, x_ref, lab_ref, out_ref,
    jbuf, ibuf, labj, labi, labcol, acc, psend, precv, weights,
    send_a, recv_a, send_b, recv_b, send_c, recv_c, send_z, recv_z, send_p, recv_p,
):
    block = lax.axis_index("block")
    piece = lax.axis_index("piece")
    z = block // NY % NZ
    y = block % NY
    x = piece // 2 * 2 + block // (NY * NZ)
    c = piece % 2

    def device(px, py, pz, pc):
        return (px % 2 * (NY * NZ) + pz * NY + py, px // 2 * 2 + pc)

    def place(a, b, core):
        return (x + a * (1 - core) + b * core) % NX, (y + a * core + b * (1 - core)) % NY

    def plane_device(a, b):
        px, py = place(a, b, c)
        return device(px, py, z, c)

    other_core = device(x, y, z, 1 - c)
    a_up, a_down = plane_device(1, 0), plane_device(3, 0)
    b_up, b_down = plane_device(0, 1), plane_device(0, 3)
    z_up, z_down = device(x, y, (z + 1) % NZ, c), device(x, y, (z + NZ - 1) % NZ, c)

    def unit(rows, labels, source, target, sends, recvs, key, to, first=0, count=ROWS):
        def copy(kind, source_ref, target_ref):
            return pltpu.make_async_remote_copy(
                src_ref=source_ref,
                dst_ref=target_ref,
                send_sem=sends.at[(kind, *key)],
                recv_sem=recvs.at[(kind, *key)],
                device_id=to,
                device_id_type=MESH,
            )

        copies = [copy(0, rows.at[source, pl.ds(first, count)], rows.at[target, pl.ds(first, count)])]
        if first == 0:
            copies.append(copy(1, labels.at[source], labels.at[target]))
        return copies

    started = []

    def send(make, *args):
        for copy in make(*args):
            copy.start()
        started.append((make, args))

    def arrived(copies):
        for copy in copies:
            copy.wait_recv()

    def along_a(source, target, to, key, first=0, count=ROWS):
        return unit(
            jbuf, labj, ORDER[source, OWN, 0], ORDER[target, OWN, 0], send_a, recv_a, (key,), to, first, count
        )

    def along_b(a, source, target, to, key, first=0, count=ROWS):
        return unit(
            jbuf, labj, ORDER[a, source, 0], ORDER[a, target, 0], send_b, recv_b, (a, key), to, first, count
        )

    def to_core(a, b):
        return unit(jbuf, labj, ORDER[a, b, 0], ORDER[a, b, 1], send_c, recv_c, (a, b), other_core)

    def along_z(source, target, to, half):
        return unit(
            ibuf, labi, z_slot(source), z_slot(target), send_z, recv_z, (z_slot(target), half), to,
            half * HALF, HALF,
        )

    live_rows = lax.broadcasted_iota(jnp.int32, (ROWS, 1), 0) // HALF < count_ref[0, 0]
    own = jnp.where(live_rows, x_ref[...], 0.0).astype(jnp.bfloat16)
    jbuf[0] = own
    ibuf[0] = own
    labj[0] = lab_ref[...]
    labi[0] = lab_ref[...]

    barrier = pltpu.get_barrier_semaphore()
    for neighbour in (a_up, a_down, b_up, b_down, z_up, z_down, other_core):
        pl.semaphore_signal(barrier, inc=1, device_id=neighbour, device_id_type=MESH)
    pl.semaphore_wait(barrier, 7)

    def open_b(a):
        send(along_b, a, OWN, LAST, b_up, 0)
        send(along_b, a, OWN, NEXT, b_down, 1)
        send(to_core, a, OWN)

    def near_b(a):
        arrived(along_b(a, OWN, LAST, b_up, 0))
        send(along_b, a, LAST, FAR, b_up, 2, 0, HALF)
        arrived(along_b(a, OWN, NEXT, b_down, 1))
        send(along_b, a, NEXT, FAR, b_down, 3, HALF, HALF)
        send(to_core, a, LAST)
        send(to_core, a, NEXT)

    def far_b(a):
        arrived(along_b(a, LAST, FAR, b_up, 2, 0, HALF))
        arrived(along_b(a, NEXT, FAR, b_down, 3, HALF, HALF))
        send(to_core, a, FAR)

    def near_a():
        arrived(along_a(OWN, LAST, a_up, 0))
        send(along_a, LAST, FAR, a_up, 2, 0, HALF)
        arrived(along_a(OWN, NEXT, a_down, 1))
        send(along_a, NEXT, FAR, a_down, 3, HALF, HALF)
        open_b(LAST)
        open_b(NEXT)

    def far_a():
        arrived(along_a(LAST, FAR, a_up, 2, 0, HALF))
        arrived(along_a(NEXT, FAR, a_down, 3, HALF, HALF))
        open_b(FAR)

    def z_arrives(step, half):
        arrived(along_z(1 - step, -step, z_up, half))
        if step < 3:
            send(along_z, -step, -step - 1, z_up, half)
        elif half == 0:
            send(along_z, -3, 4, z_up, 0)
        arrived(along_z(step - 1, step, z_down, half))
        if step < 3:
            send(along_z, step, step + 1, z_down, half)
        elif half == 1:
            send(along_z, 3, 4, z_down, 1)

    def z_far():
        arrived(along_z(-3, 4, z_up, 0))
        arrived(along_z(3, 4, z_down, 1))

    def core_arrives(chunk):
        for a, b in CHUNKS[chunk]:
            arrived(to_core(a, b))

    send(along_a, OWN, LAST, a_up, 0)
    send(along_a, OWN, NEXT, a_down, 1)
    for half in range(2):
        send(along_z, 0, -1, z_up, half)
        send(along_z, 0, 1, z_down, half)
    open_b(OWN)

    factor = 0.5 * math.sqrt(jbuf.shape[-1] / (ROWS * NX * NY * NZ * 2)) / 8.0 * scale_ref[0]
    half_scale = 0.5 * scale_ref[0]
    half_offset = 0.5 * offset_ref[0]

    for (a, b, core), place_in_plane in ORDER.items():
        px, py = place(OFFSETS[a], OFFSETS[b], 1 - c if core else c)
        column_block = px % 2 * (NY * NZ) + z * NY + py

        @pl.loop(0, NZ)
        def _(i, j=place_in_plane, column_block=column_block):
            step = (i % 2) * ((i + 1) // 2) + (1 - i % 2) * (NZ - i // 2)
            row_block = x % 2 * (NY * NZ) + (z + step) % NZ * NY + y
            weights[i, j] = factor * mult_ref[row_block, column_block].astype(jnp.float32)

    def coefficients(scores, same, size):
        return size * jnp.tanh(half_scale * scores + half_offset) + jnp.where(same, -size, size)

    acc[...] = jnp.zeros_like(acc)
    scores = lax.dot_general(own, own, (((1,), (1,)), ((), ())), preferred_element_type=jnp.float32)
    square = (ROWS, ROWS)
    eye = lax.broadcasted_iota(jnp.int32, square, 0) == lax.broadcasted_iota(jnp.int32, square, 1)
    diagonal = jnp.where(eye, coefficients(scores, jnp.full(square, True), weights[0, 0]), 0.0)
    acc[0] = -jnp.dot(diagonal.astype(jnp.bfloat16), own, preferred_element_type=jnp.float32)

    def partial(direction, step, half):
        return [
            pltpu.make_async_remote_copy(
                src_ref=psend.at[direction, step, half],
                dst_ref=precv.at[direction, step, half],
                send_sem=send_p.at[direction, step, half],
                recv_sem=recv_p.at[direction, step, half],
                device_id=z_down if direction else z_up,
                device_id_type=MESH,
            )
        ]

    def pass_on(direction, step, half):
        row = z_slot(4 if step == 0 else step - 4 if direction else 4 - step)
        value = acc[row, half * HALF : (half + 1) * HALF]
        if step >= 2 or (step == 1 and half == direction):
            arrived(partial(direction, step - 1, half))
            value = value + precv[direction, step - 1, half].astype(jnp.float32)
        psend[direction, step, half] = value.astype(jnp.bfloat16)
        send(partial, direction, step, half)

    def label_columns(pair):
        for i in (2 * pair, 2 * pair + 1):
            labcol[i] = jnp.broadcast_to(labi[i].astype(jnp.float32), square).T

    near_a()
    z_arrives(1, 0)
    near_b(OWN)
    z_arrives(1, 1)

    def before(step):
        if step == 0:
            core_arrives(0)
            label_columns(0)
        if step == 1:
            z_arrives(2, 0)
            far_a()
            near_b(LAST)
            z_arrives(2, 1)
            label_columns(1)
        if step == 2:
            near_b(NEXT)
            core_arrives(1)
        if step == 3:
            far_b(OWN)
            z_arrives(3, 0)
        if step == 4:
            far_b(NEXT)
            z_arrives(3, 1)
            core_arrives(2)
        if step == 5:
            near_b(FAR)
        if step == 6:
            label_columns(2)
        if step == 7:
            far_b(LAST)
        if step == 8:
            far_b(FAR)
        if step == 9:
            z_far()
            label_columns(3)
        if step == 12:
            core_arrives(3)
        if step == 13:
            pass_on(0, 0, 0)
            pass_on(1, 0, 1)
            pass_on(1, 1, 0)
        if step == 14:
            pass_on(0, 1, 1)

    width = jbuf.shape[-1]

    @pl.loop(0, len(STEPS))
    def _(step):
        pair = step * 0
        chunk = step * 0
        for s, (p, k) in enumerate(STEPS):
            pair = jnp.where(step == s, p, pair)
            chunk = jnp.where(step == s, k, chunk)

            @pl.when(step == s)
            def _(s=s):
                before(s)

        if not COMPUTE:
            return
        columns = jbuf[pl.ds(chunk * 8, 8)].reshape(8 * ROWS, width)
        rows = ibuf[pl.ds(pair * 2, 2)].reshape(2 * ROWS, width)
        scores = lax.dot_general(
            rows, columns, (((1,), (1,)), ((), ())), preferred_element_type=jnp.float32
        )
        lines = []
        for u in range(2):
            parts = []
            for q in range(8):
                same = labcol[pair * 2 + u] == labj[chunk * 8 + q].astype(jnp.float32)
                part = scores[u * ROWS : (u + 1) * ROWS, q * ROWS : (q + 1) * ROWS]
                size = weights[pair * 2 + u, chunk * 8 + q]
                parts.append(coefficients(part, same, size).astype(jnp.bfloat16))
            lines.append(jnp.concatenate(parts, axis=1))
        grads = jnp.dot(
            jnp.concatenate(lines, axis=0), columns, preferred_element_type=jnp.float32
        )
        for u in range(2):
            acc[pair * 2 + u] += grads[u * ROWS : (u + 1) * ROWS]

    pass_on(0, 1, 0)
    pass_on(1, 1, 1)
    for step in (2, 3):
        for half in range(2):
            pass_on(0, step, 1 - half)
            pass_on(1, step, half)
    for half in range(2):
        arrived(partial(0, 3, half))
        arrived(partial(1, 3, half))
        rows = slice(half * HALF, (half + 1) * HALF)
        total = (
            acc[0, rows]
            + precv[0, 3, half].astype(jnp.float32)
            + precv[1, 3, half].astype(jnp.float32)
        )
        out_ref[rows, :] = jnp.where(live_rows[rows], total, 0.0)
    for make, args in started:
        for copy in make(*args):
            copy.wait_send()


def shards(rows, labels, counts, multiplicity, scaling, offset):
    width = rows.shape[1]
    smem = pl.BlockSpec(memory_space=pltpu.SMEM)
    vmem = pl.BlockSpec(memory_space=pltpu.VMEM)
    dma = pltpu.SemaphoreType.DMA
    return pl.pallas_call(
        kernel,
        out_shape=jax.ShapeDtypeStruct((ROWS, width), jnp.float32),
        in_specs=[smem, smem, smem, smem, vmem, vmem],
        out_specs=vmem,
        scratch_shapes=[
            pltpu.VMEM((32, ROWS, width), jnp.bfloat16),
            pltpu.VMEM((NZ, ROWS, width), jnp.bfloat16),
            pltpu.VMEM((32, 1, ROWS), jnp.int32),
            pltpu.VMEM((NZ, 1, ROWS), jnp.int32),
            pltpu.VMEM((NZ, ROWS, ROWS), jnp.float32),
            pltpu.VMEM((NZ, ROWS, width), jnp.float32),
            pltpu.VMEM((2, 4, 2, HALF, width), jnp.bfloat16),
            pltpu.VMEM((2, 4, 2, HALF, width), jnp.bfloat16),
            pltpu.SMEM((NZ, 32), jnp.float32),
            dma((2, 4)), dma((2, 4)), dma((2, 4, 4)), dma((2, 4, 4)), dma((2, 4, 4)), dma((2, 4, 4)),
            dma((2, 8, 2)), dma((2, 8, 2)), dma((2, 4, 2)), dma((2, 4, 2)),
        ],
        compiler_params=pltpu.CompilerParams(
            collective_id=0, has_side_effects=True, vmem_limit_bytes=VMEM_MIB * 1024 * 1024
        ),
    )(multiplicity, scaling, offset, counts, rows, labels.reshape(1, ROWS))


def solution(mesh):
    return jax.shard_map(
        shards,
        mesh=mesh,
        in_specs=(
            P(("block", "piece"), None),
            P(("block", "piece")),
            P("block", "piece"),
            P(),
            P(),
            P(),
        ),
        out_specs=P(("block", "piece"), None),
        check_vma=False,
    )
```

```python
import math

import jax
import jax.numpy as jnp
from jax import lax
from jax.experimental import pallas as pl
from jax.experimental.pallas import tpu as pltpu
from jax.sharding import PartitionSpec as P

MESH = pl.DeviceIdType.MESH
ROWS = 128
HALF = 64
NX, NY, NZ = 4, 4, 8
COMPUTE = True
VMEM_MIB = 60

OFFSETS = (0, 1, 3, 2)
OWN, NEXT, LAST, FAR = range(4)


def z_slot(step):
    return 2 * step - 1 if step > 0 else -2 * step


CHUNKS = (
    ((0, 0), (2, 0), (1, 0), (0, 2)),
    ((0, 1), (3, 0), (0, 3), (2, 2)),
    ((2, 1), (1, 2), (1, 1), (3, 1)),
    ((3, 2), (2, 3), (1, 3), (3, 3)),
)
ORDER = {}
for _chunk, _units in enumerate(CHUNKS):
    for _i, _unit in enumerate(_units):
        for _core in range(2):
            ORDER[(*_unit, _core)] = 8 * _chunk + 2 * _i + _core

A, B, C, Z, T, R = range(6)
PROGRAM = (
    (A, 2, 0), (A, 1, 1), (A, 2, 1), (A, 1, 0), (Z, -1, 0), (Z, 1, 1), (Z, -1, 1), (Z, 1, 0),
    (B, 0, 2, 0), (B, 0, 1, 1), (B, 0, 2, 1), (B, 0, 1, 0), (C, 0, 0), (A, 3, 0), (A, 3, 1),
    (B, 2, 2, 0), (B, 2, 1, 0), (B, 1, 1, 1), (B, 1, 2, 1), (Z, -2, 0), (Z, 2, 1), (B, 0, 3, 0),
    (B, 0, 3, 1), (B, 2, 1, 1), (B, 2, 2, 1), (B, 1, 2, 0), (B, 1, 1, 0), (C, 2, 0), (C, 1, 0),
    (Z, -2, 1), (Z, 2, 0), (C, 0, 2), (C, 0, 1), (T, 0, 0), (Z, -3, 0), (Z, 3, 1), (B, 2, 3, 0),
    (B, 3, 2, 0), (B, 3, 1, 1), (B, 3, 2, 1), (B, 3, 1, 0), (C, 3, 0), (B, 1, 3, 1), (C, 0, 3),
    (Z, -3, 1), (Z, 3, 0), (T, 1, 0), (B, 2, 3, 1), (C, 2, 2), (C, 2, 1), (B, 1, 3, 0), (C, 1, 2),
    (C, 1, 1), (Z, 4, 0), (Z, 4, 1), (T, 1, 1), (B, 3, 3, 1), (T, 0, 1), (B, 3, 3, 0), (C, 3, 1),
    (T, 2, 0), (C, 3, 2), (T, 2, 1), (C, 2, 3), (C, 1, 3), (T, 3, 0), (C, 3, 3), (T, 3, 1), (T, 3, 2),
    (T, 3, 3), (R, 0, 0, 0), (R, 1, 0, 1), (R, 1, 1, 0), (T, 2, 2), (T, 2, 3), (R, 0, 1, 1),
    (R, 0, 1, 0), (R, 1, 1, 1), (T, 1, 2), (T, 1, 3), (R, 1, 2, 0), (R, 0, 2, 1), (T, 0, 2), (T, 0, 3),
    (R, 0, 2, 0), (R, 1, 2, 1), (R, 1, 3, 0), (R, 0, 3, 1), (R, 1, 3, 1), (R, 0, 3, 0), (R, 1, 4, 0),
    (R, 0, 4, 1), (R, 1, 4, 1), (R, 0, 4, 0),
)
STEPS = tuple(entry[1:] for entry in PROGRAM if entry[0] == T)


def upward(entry):
    if entry[0] == Z:
        return entry[1] < 0 or (entry[1] == 4 and entry[2] == 0)
    return entry[-2] == LAST or (entry[-2] == FAR and entry[-1] == 0)


def needs(entry):
    kind, half = entry[0], entry[-1]
    if kind in (A, B) and entry[-2] == FAR:
        return [(*entry[:-2], NEXT if half else LAST, half)]
    if kind == B:
        return [(A, entry[1], half)] if entry[1] != OWN else []
    if kind == C:
        a, b = entry[1:]
        unit = (B, a, b) if b != OWN else (A, a)
        return [(*unit, half) for half in range(2)] if (a, b) != (OWN, OWN) else []
    if kind == Z:
        source = z_source(entry)
        return [(Z, source, half)] if source else []
    if kind == T:
        steps = [step for step in range(-3, 5) if step and z_slot(step) // 2 == entry[1]]
        lines = [need for unit in CHUNKS[entry[2]] for need in (*needs((C, *unit)), (C, *unit))]
        return [(Z, step, half) for step in steps for half in range(2)] + lines
    return []


def z_source(entry):
    step, half = entry[1:]
    if step == 4:
        return 3 if half else -3
    return step - 1 if step > 0 else step + 1


def carries_label(entry):
    if entry[0] == C:
        return True
    if entry[0] == Z and entry[1] != 4 or entry[0] != Z and entry[-2] != FAR:
        return entry[-1] == (0 if upward(entry) else 1)
    return entry[-1] == 0


def kernel(
    mult_ref, scale_ref, offset_ref, count_ref, x_ref, lab_ref, out_ref,
    jbuf, ibuf, labj, labi, labcol, acc, psend, precv, weights,
    send_a, recv_a, send_b, recv_b, send_c, recv_c, send_z, recv_z,
    lsend_a, lrecv_a, lsend_b, lrecv_b, lsend_c, lrecv_c, lsend_z, lrecv_z, send_p, recv_p,
):
    block = lax.axis_index("block")
    piece = lax.axis_index("piece")
    z = block // NY % NZ
    y = block % NY
    x = piece // 2 * 2 + block // (NY * NZ)
    c = piece % 2

    def device(px, py, pz, pc):
        return (px % 2 * (NY * NZ) + pz * NY + py, px // 2 * 2 + pc)

    def place(a, b, core):
        return (x + a * (1 - core) + b * core) % NX, (y + a * core + b * (1 - core)) % NY

    def plane_device(a, b):
        px, py = place(a, b, c)
        return device(px, py, z, c)

    other_core = device(x, y, z, 1 - c)
    a_up, a_down = plane_device(1, 0), plane_device(3, 0)
    b_up, b_down = plane_device(0, 1), plane_device(0, 3)
    z_up, z_down = device(x, y, (z + 1) % NZ, c), device(x, y, (z + NZ - 1) % NZ, c)

    def copies(entry):
        kind, half = entry[0], entry[-1]
        rows, labels, part = jbuf, labj, pl.ds(half * HALF, HALF)
        if kind in (A, B):
            unit = entry[-2]
            source = (NEXT if half else LAST) if unit == FAR else OWN
            line = (entry[1],) if kind == B else ()
            source = ORDER[(*line, source, 0)] if kind == B else ORDER[source, OWN, 0]
            target = ORDER[(*line, unit, 0)] if kind == B else ORDER[unit, OWN, 0]
            key, label_key = (*line, unit, half), (*line, unit)
            to = ((a_up, a_down), (b_up, b_down))[kind][0 if upward(entry) else 1]
            semaphores = ((send_a, recv_a, lsend_a, lrecv_a), (send_b, recv_b, lsend_b, lrecv_b))[kind]
        elif kind == C:
            a, b = entry[1:]
            source, target, part = ORDER[a, b, 0], ORDER[a, b, 1], pl.ds(0, ROWS)
            key = label_key = (a, b)
            to = other_core
            semaphores = send_c, recv_c, lsend_c, lrecv_c
        else:
            rows, labels = ibuf, labi
            source, target = z_slot(z_source(entry)), z_slot(entry[1])
            key, label_key = (target, half), (target,)
            to = z_up if upward(entry) else z_down
            semaphores = send_z, recv_z, lsend_z, lrecv_z

        def copy(source_ref, target_ref, send_sem, recv_sem):
            return pltpu.make_async_remote_copy(
                src_ref=source_ref, dst_ref=target_ref, send_sem=send_sem, recv_sem=recv_sem,
                device_id=to, device_id_type=MESH,
            )

        send, recv, lsend, lrecv = semaphores
        made = [copy(rows.at[source, part], rows.at[target, part], send.at[key], recv.at[key])]
        if carries_label(entry):
            made.append(copy(labels.at[source], labels.at[target], lsend.at[label_key], lrecv.at[label_key]))
        return made

    started = []

    def send(make, *args):
        for copy in make(*args):
            copy.start()
        started.append((make, args))

    def arrived(made):
        for copy in made:
            copy.wait_recv()

    live_rows = lax.broadcasted_iota(jnp.int32, (ROWS, 1), 0) // HALF < count_ref[0, 0]
    own = jnp.where(live_rows, x_ref[...], 0.0).astype(jnp.bfloat16)
    jbuf[0] = own
    ibuf[0] = own
    labj[0] = lab_ref[...]
    labi[0] = lab_ref[...]

    barrier = pltpu.get_barrier_semaphore()
    for neighbour in (a_up, a_down, b_up, b_down, z_up, z_down, other_core):
        pl.semaphore_signal(barrier, inc=1, device_id=neighbour, device_id_type=MESH)
    pl.semaphore_wait(barrier, 7)

    known = set()

    def take(entry):
        for need in needs(entry):
            if need not in known:
                known.add(need)
                arrived(copies(need))
        if entry[0] == R:
            pass_on(*entry[1:])
        elif entry[0] != T:
            send(copies, entry)

    first = min(i for i, entry in enumerate(PROGRAM) if needs(entry))
    for entry in PROGRAM[:first]:
        take(entry)

    factor = 0.5 * math.sqrt(jbuf.shape[-1] / (ROWS * NX * NY * NZ * 2)) / 8.0 * scale_ref[0]
    half_scale = 0.5 * scale_ref[0]
    half_offset = 0.5 * offset_ref[0]

    for (a, b, core), place_in_plane in ORDER.items():
        px, py = place(OFFSETS[a], OFFSETS[b], 1 - c if core else c)
        column_block = px % 2 * (NY * NZ) + z * NY + py

        @pl.loop(0, NZ)
        def _(i, j=place_in_plane, column_block=column_block):
            step = (i % 2) * ((i + 1) // 2) + (1 - i % 2) * (NZ - i // 2)
            row_block = x % 2 * (NY * NZ) + (z + step) % NZ * NY + y
            weights[i, j] = factor * mult_ref[row_block, column_block].astype(jnp.float32)

    def coefficients(scores, same, size):
        return size * jnp.tanh(half_scale * scores + half_offset) + jnp.where(same, -size, size)

    acc[...] = jnp.zeros_like(acc)
    scores = lax.dot_general(own, own, (((1,), (1,)), ((), ())), preferred_element_type=jnp.float32)
    square = (ROWS, ROWS)
    eye = lax.broadcasted_iota(jnp.int32, square, 0) == lax.broadcasted_iota(jnp.int32, square, 1)
    diagonal = jnp.where(eye, coefficients(scores, jnp.full(square, True), weights[0, 0]), 0.0)
    acc[0] = -jnp.dot(diagonal.astype(jnp.bfloat16), own, preferred_element_type=jnp.float32)

    def partial(direction, step, half):
        return [
            pltpu.make_async_remote_copy(
                src_ref=psend.at[direction, step, half],
                dst_ref=precv.at[direction, step, half],
                send_sem=send_p.at[direction, step, half],
                recv_sem=recv_p.at[direction, step, half],
                device_id=z_down if direction else z_up,
                device_id_type=MESH,
            )
        ]

    def pass_on(direction, step, half):
        row = z_slot(4 if step == 0 else step - 4 if direction else 4 - step)
        rows = slice(half * HALF, (half + 1) * HALF)
        value = acc[row, rows]
        if step == 4:
            if direction not in met[half]:
                arrived(partial(direction, 3, half))
                met[half].append(direction)
            if len(met[half]) == 2:
                for way in range(2):
                    value = value + precv[way, 3, half].astype(jnp.float32)
                out_ref[rows, :] = jnp.where(live_rows[rows], value, 0.0)
            return
        if step >= 2 or (step == 1 and half == direction):
            arrived(partial(direction, step - 1, half))
            value = value + precv[direction, step - 1, half].astype(jnp.float32)
        psend[direction, step, half] = value.astype(jnp.bfloat16)
        send(partial, direction, step, half)

    met = ([], [])

    def label_columns(pair):
        for i in (2 * pair, 2 * pair + 1):
            labcol[i] = jnp.broadcast_to(labi[i].astype(jnp.float32), square).T

    groups, group, pairs_met = [], [], set()
    for entry in PROGRAM[first:]:
        group.append(entry)
        if entry[0] == T:
            groups.append(group)
            group = []

    def before(entries):
        for entry in entries:
            take(entry)
            if entry[0] == T and entry[1] not in pairs_met:
                pairs_met.add(entry[1])
                label_columns(entry[1])

    before(groups[0])

    width = jbuf.shape[-1]

    @pl.loop(0, len(STEPS))
    def _(step):
        pair = step * 0
        chunk = step * 0
        for s, (p, k) in enumerate(STEPS):
            pair = jnp.where(step == s, p, pair)
            chunk = jnp.where(step == s, k, chunk)

            if s == 0:
                continue

            @pl.when(step == s)
            def _(s=s):
                before(groups[s])

        if not COMPUTE:
            return
        columns = jbuf[pl.ds(chunk * 8, 8)].reshape(8 * ROWS, width)
        rows = ibuf[pl.ds(pair * 2, 2)].reshape(2 * ROWS, width)
        scores = lax.dot_general(
            rows, columns, (((1,), (1,)), ((), ())), preferred_element_type=jnp.float32
        )
        lines = []
        for u in range(2):
            parts = []
            for q in range(8):
                same = labcol[pair * 2 + u] == labj[chunk * 8 + q].astype(jnp.float32)
                part = scores[u * ROWS : (u + 1) * ROWS, q * ROWS : (q + 1) * ROWS]
                size = weights[pair * 2 + u, chunk * 8 + q]
                parts.append(coefficients(part, same, size).astype(jnp.bfloat16))
            lines.append(jnp.concatenate(parts, axis=1))
        grads = jnp.dot(
            jnp.concatenate(lines, axis=0), columns, preferred_element_type=jnp.float32
        )
        for u in range(2):
            acc[pair * 2 + u] += grads[u * ROWS : (u + 1) * ROWS]

    before(group)
    for make, args in started:
        for copy in make(*args):
            copy.wait_send()


def shards(rows, labels, counts, multiplicity, scaling, offset):
    width = rows.shape[1]
    smem = pl.BlockSpec(memory_space=pltpu.SMEM)
    vmem = pl.BlockSpec(memory_space=pltpu.VMEM)
    dma = pltpu.SemaphoreType.DMA
    return pl.pallas_call(
        kernel,
        out_shape=jax.ShapeDtypeStruct((ROWS, width), jnp.float32),
        in_specs=[smem, smem, smem, smem, vmem, vmem],
        out_specs=vmem,
        scratch_shapes=[
            pltpu.VMEM((32, ROWS, width), jnp.bfloat16),
            pltpu.VMEM((NZ, ROWS, width), jnp.bfloat16),
            pltpu.VMEM((32, 1, ROWS), jnp.int32),
            pltpu.VMEM((NZ, 1, ROWS), jnp.int32),
            pltpu.VMEM((NZ, ROWS, ROWS), jnp.float32),
            pltpu.VMEM((NZ, ROWS, width), jnp.float32),
            pltpu.VMEM((2, 4, 2, HALF, width), jnp.bfloat16),
            pltpu.VMEM((2, 4, 2, HALF, width), jnp.bfloat16),
            pltpu.SMEM((NZ, 32), jnp.float32),
            *(dma(shape) for shape in ((4, 2), (4, 4, 2), (4, 4), (NZ, 2)) for _ in range(2)),
            *(dma(shape) for shape in ((4,), (4, 4), (4, 4), (NZ,)) for _ in range(2)),
            dma((2, 4, 2)), dma((2, 4, 2)),
        ],
        compiler_params=pltpu.CompilerParams(
            collective_id=0, has_side_effects=True, vmem_limit_bytes=VMEM_MIB * 1024 * 1024
        ),
    )(multiplicity, scaling, offset, counts, rows, labels.reshape(1, ROWS))


def solution(mesh):
    return jax.shard_map(
        shards,
        mesh=mesh,
        in_specs=(
            P(("block", "piece"), None),
            P(("block", "piece")),
            P("block", "piece"),
            P(),
            P(),
            P(),
        ),
        out_specs=P(("block", "piece"), None),
        check_vma=False,
    )
```

```python
import math

import jax
import jax.numpy as jnp
from jax import lax
from jax.experimental import pallas as pl
from jax.experimental.pallas import tpu as pltpu
from jax.sharding import PartitionSpec as P

MESH = pl.DeviceIdType.MESH
ROWS = 128
HALF = 64
NX, NY, NZ = 4, 4, 8
COMPUTE = True
REDUCE = True
OUT_VMEM = True
VMEM_MIB = 60

OFFSETS = (0, 1, 3, 2)
OWN, NEXT, LAST, FAR = range(4)


def z_slot(step):
    return 2 * step - 1 if step > 0 else -2 * step


CHUNKS = (
    ((0, 0), (2, 0), (1, 0), (0, 2)),
    ((0, 1), (3, 0), (0, 3), (2, 2)),
    ((2, 1), (1, 2), (1, 1), (3, 1)),
    ((3, 2), (2, 3), (1, 3), (3, 3)),
)
ORDER = {}
for _chunk, _units in enumerate(CHUNKS):
    for _i, _unit in enumerate(_units):
        for _core in range(2):
            ORDER[(*_unit, _core)] = 8 * _chunk + 2 * _i + _core

A, B, C, Z, T, R = range(6)
PROGRAM = (
    (A, 2, 0), (A, 1, 1), (A, 2, 1), (A, 1, 0), (Z, -1, 0), (Z, 1, 1), (Z, -1, 1), (Z, 1, 0),
    (B, 0, 2, 0), (B, 0, 1, 1), (B, 0, 2, 1), (B, 0, 1, 0), (C, 0, 0), (A, 3, 0), (A, 3, 1),
    (B, 2, 2, 0), (B, 2, 1, 0), (B, 1, 1, 1), (B, 1, 2, 1), (Z, -2, 0), (Z, 2, 1), (B, 0, 3, 0),
    (B, 0, 3, 1), (B, 2, 1, 1), (B, 2, 2, 1), (B, 1, 2, 0), (B, 1, 1, 0), (C, 2, 0), (C, 1, 0),
    (Z, -2, 1), (Z, 2, 0), (C, 0, 2), (C, 0, 1), (T, 1, 0), (Z, -3, 0), (Z, 3, 1), (B, 2, 3, 0),
    (B, 3, 2, 0), (B, 3, 1, 1), (B, 3, 2, 1), (B, 3, 1, 0), (C, 3, 0), (T, 0, 0), (B, 1, 3, 1),
    (C, 0, 3), (Z, -3, 1), (Z, 3, 0), (T, 2, 0), (B, 2, 3, 1), (C, 2, 2), (C, 2, 1), (B, 1, 3, 0),
    (C, 1, 2), (C, 1, 1), (Z, 4, 0), (Z, 4, 1), (T, 2, 1), (B, 3, 3, 1), (T, 1, 1), (B, 3, 3, 0),
    (C, 3, 1), (T, 3, 0), (C, 3, 2), (T, 3, 1), (C, 2, 3), (C, 1, 3), (T, 4, 0), (C, 3, 3), (T, 4, 1),
    (T, 4, 2), (T, 4, 3), (R, 0, 0, 0), (R, 1, 0, 1), (T, 3, 2), (T, 3, 3), (R, 1, 1, 0), (R, 0, 1, 1),
    (R, 0, 1, 0), (R, 1, 1, 1), (T, 2, 2), (T, 2, 3), (R, 1, 2, 0), (R, 0, 2, 1), (T, 1, 2), (T, 1, 3),
    (R, 0, 2, 0), (R, 1, 2, 1), (T, 0, 1), (T, 0, 2), (R, 0, 3, 1), (R, 1, 3, 0), (T, 0, 3),
    (R, 1, 3, 1), (R, 0, 3, 0), (R, 1, 4, 0), (R, 0, 4, 1), (R, 1, 4, 1), (R, 0, 4, 0),
)
STEPS = tuple(entry[1:] for entry in PROGRAM if entry[0] == T)


def upward(entry):
    if entry[0] == Z:
        return entry[1] < 0 or (entry[1] == 4 and entry[2] == 0)
    return entry[-2] == LAST or (entry[-2] == FAR and entry[-1] == 0)


def needs(entry):
    kind, half = entry[0], entry[-1]
    if kind in (A, B) and entry[-2] == FAR:
        return [(*entry[:-2], NEXT if half else LAST, half)]
    if kind == B:
        return [(A, entry[1], half)] if entry[1] != OWN else []
    if kind == C:
        a, b = entry[1:]
        unit = (B, a, b) if b != OWN else (A, a)
        return [(*unit, half) for half in range(2)] if (a, b) != (OWN, OWN) else []
    if kind == Z:
        source = z_source(entry)
        return [(Z, source, half)] if source else []
    if kind == T:
        steps = [step for step in range(-3, 5) if step and abs(step) == entry[1]]
        lines = [need for unit in CHUNKS[entry[2]] for need in (*needs((C, *unit)), (C, *unit))]
        return [(Z, step, half) for step in steps for half in range(2)] + lines
    return []


def z_source(entry):
    step, half = entry[1:]
    if step == 4:
        return 3 if half else -3
    return step - 1 if step > 0 else step + 1


def carries_label(entry):
    if entry[0] == C:
        return True
    if entry[0] == Z and entry[1] != 4 or entry[0] != Z and entry[-2] != FAR:
        return entry[-1] == (0 if upward(entry) else 1)
    return entry[-1] == 0


def kernel(
    mult_ref, scale_ref, offset_ref, count_ref, x_ref, lab_ref, out_ref,
    jbuf, ibuf, labj, labi, labcol, acc, psend, precv, row_blocks, column_blocks,
    send_a, recv_a, send_b, recv_b, send_c, recv_c, send_z, recv_z,
    lsend_a, lrecv_a, lsend_b, lrecv_b, lsend_c, lrecv_c, lsend_z, lrecv_z, send_p, recv_p,
):
    block = lax.axis_index("block")
    piece = lax.axis_index("piece")
    z = block // NY % NZ
    y = block % NY
    x = piece // 2 * 2 + block // (NY * NZ)
    c = piece % 2

    def device(px, py, pz, pc):
        return (px % 2 * (NY * NZ) + pz * NY + py, px // 2 * 2 + pc)

    def place(a, b, core):
        return (x + a * (1 - core) + b * core) % NX, (y + a * core + b * (1 - core)) % NY

    def plane_device(a, b):
        px, py = place(a, b, c)
        return device(px, py, z, c)

    other_core = device(x, y, z, 1 - c)
    a_up, a_down = plane_device(1, 0), plane_device(3, 0)
    b_up, b_down = plane_device(0, 1), plane_device(0, 3)
    z_up, z_down = device(x, y, (z + 1) % NZ, c), device(x, y, (z + NZ - 1) % NZ, c)

    def copies(entry):
        kind, half = entry[0], entry[-1]
        rows, labels, part = jbuf, labj, pl.ds(half * HALF, HALF)
        if kind in (A, B):
            unit = entry[-2]
            source = (NEXT if half else LAST) if unit == FAR else OWN
            line = (entry[1],) if kind == B else ()
            source = ORDER[(*line, source, 0)] if kind == B else ORDER[source, OWN, 0]
            target = ORDER[(*line, unit, 0)] if kind == B else ORDER[unit, OWN, 0]
            key, label_key = (*line, unit, half), (*line, unit)
            to = ((a_up, a_down), (b_up, b_down))[kind][0 if upward(entry) else 1]
            semaphores = ((send_a, recv_a, lsend_a, lrecv_a), (send_b, recv_b, lsend_b, lrecv_b))[kind]
        elif kind == C:
            a, b = entry[1:]
            source, target, part = ORDER[a, b, 0], ORDER[a, b, 1], pl.ds(0, ROWS)
            key = label_key = (a, b)
            to = other_core
            semaphores = send_c, recv_c, lsend_c, lrecv_c
        else:
            rows, labels = ibuf, labi
            source, target = z_slot(z_source(entry)), z_slot(entry[1])
            key, label_key = (target, half), (target,)
            to = z_up if upward(entry) else z_down
            semaphores = send_z, recv_z, lsend_z, lrecv_z

        def copy(source_ref, target_ref, send_sem, recv_sem):
            return pltpu.make_async_remote_copy(
                src_ref=source_ref, dst_ref=target_ref, send_sem=send_sem, recv_sem=recv_sem,
                device_id=to, device_id_type=MESH,
            )

        send, recv, lsend, lrecv = semaphores
        made = [copy(rows.at[source, part], rows.at[target, part], send.at[key], recv.at[key])]
        if carries_label(entry):
            made.append(copy(labels.at[source], labels.at[target], lsend.at[label_key], lrecv.at[label_key]))
        return made

    started = []

    def send(make, *args):
        for copy in make(*args):
            copy.start()
        started.append((make, args))

    def arrived(made):
        for copy in made:
            copy.wait_recv()

    barrier = pltpu.get_barrier_semaphore()
    for neighbour in (a_up, a_down, b_up, b_down, z_up, z_down, other_core):
        pl.semaphore_signal(barrier, inc=1, device_id=neighbour, device_id_type=MESH)

    live_rows = lax.broadcasted_iota(jnp.int32, (ROWS, 1), 0) // HALF < count_ref[0, 0]
    own = jnp.where(live_rows, x_ref[...], 0.0).astype(jnp.bfloat16)
    jbuf[0] = own
    ibuf[0] = own
    labj[0] = lab_ref[...]
    labi[0] = lab_ref[...]

    pl.semaphore_wait(barrier, 7)

    known = set()

    def take(entry):
        for need in needs(entry):
            if need not in known:
                known.add(need)
                arrived(copies(need))
        if entry[0] == R:
            pass_on(*entry[1:])
        elif entry[0] != T:
            send(copies, entry)

    first = min(i for i, entry in enumerate(PROGRAM) if needs(entry))
    for entry in PROGRAM[:first]:
        take(entry)

    factor = 0.5 * math.sqrt(jbuf.shape[-1] / (ROWS * NX * NY * NZ * 2)) / 8.0 * scale_ref[0]
    half_scale = 0.5 * scale_ref[0]
    half_offset = 0.5 * offset_ref[0]

    for step in range(-3, 5):
        row_blocks[z_slot(step)] = x % 2 * (NY * NZ) + (z + NZ + step) % NZ * NY + y
    for (a, b, core), place_in_plane in ORDER.items():
        px, py = place(OFFSETS[a], OFFSETS[b], 1 - c if core else c)
        column_blocks[place_in_plane] = px % 2 * (NY * NZ) + z * NY + py

    def size_of(row, column):
        return factor * mult_ref[row_blocks[row], column_blocks[column]].astype(jnp.float32)

    def coefficients(scores, same, size):
        return size * jnp.tanh(half_scale * scores + half_offset) + jnp.where(same, -size, size)

    acc[...] = jnp.zeros_like(acc)
    scores = lax.dot_general(own, own, (((1,), (1,)), ((), ())), preferred_element_type=jnp.float32)
    square = (ROWS, ROWS)
    eye = lax.broadcasted_iota(jnp.int32, square, 0) == lax.broadcasted_iota(jnp.int32, square, 1)
    diagonal = jnp.where(eye, coefficients(scores, jnp.full(square, True), size_of(0, 0)), 0.0)
    acc[0] = -jnp.dot(diagonal.astype(jnp.bfloat16), own, preferred_element_type=jnp.float32)

    def partial(direction, step, half):
        return [
            pltpu.make_async_remote_copy(
                src_ref=psend.at[direction, step, half],
                dst_ref=precv.at[direction, step, half],
                send_sem=send_p.at[direction, step, half],
                recv_sem=recv_p.at[direction, step, half],
                device_id=z_down if direction else z_up,
                device_id_type=MESH,
            )
        ]

    def pass_on(direction, step, half):
        if not REDUCE:
            return
        row = z_slot(4 if step == 0 else step - 4 if direction else 4 - step)
        rows = slice(half * HALF, (half + 1) * HALF)
        value = acc[row, rows]
        if step == 4:
            if direction not in met[half]:
                arrived(partial(direction, 3, half))
                met[half].append(direction)
            if len(met[half]) == 2:
                for way in range(2):
                    value = value + precv[way, 3, half].astype(jnp.float32)
                out_ref[rows, :] = jnp.where(live_rows[rows], value, 0.0)
            return
        if step >= 2 or (step == 1 and half == direction):
            arrived(partial(direction, step - 1, half))
            value = value + precv[direction, step - 1, half].astype(jnp.float32)
        psend[direction, step, half] = value.astype(jnp.bfloat16)
        send(partial, direction, step, half)

    met = ([], [])

    def label_columns(distance):
        for i in {z_slot(distance), z_slot(-distance if distance < 4 else 4)}:
            labcol[i] = jnp.broadcast_to(labi[i].astype(jnp.float32), square).T

    groups, group, met_distances = [], [], set()
    for entry in PROGRAM[first:]:
        group.append(entry)
        if entry[0] == T:
            groups.append(group)
            group = []

    def before(entries):
        for entry in entries:
            take(entry)
            if entry[0] == T and entry[1] not in met_distances:
                met_distances.add(entry[1])
                label_columns(entry[1])

    before(groups[0])

    width = jbuf.shape[-1]

    @pl.loop(0, len(STEPS))
    def _(step):
        distance = step * 0
        chunk = step * 0
        for s, (p, k) in enumerate(STEPS):
            distance = jnp.where(step == s, p, distance)
            chunk = jnp.where(step == s, k, chunk)

            if s == 0:
                continue

            @pl.when(step == s)
            def _(s=s):
                before(groups[s])

        if not COMPUTE:
            return
        def multiply(first, count):
            columns = jbuf[pl.ds(chunk * 8, 8)].reshape(8 * ROWS, width)
            rows = ibuf[pl.ds(first, count)].reshape(count * ROWS, width)
            scores = lax.dot_general(
                rows, columns, (((1,), (1,)), ((), ())), preferred_element_type=jnp.float32
            )
            lines = []
            for u in range(count):
                parts = []
                for q in range(8):
                    same = labcol[first + u] == labj[chunk * 8 + q].astype(jnp.float32)
                    part = scores[u * ROWS : (u + 1) * ROWS, q * ROWS : (q + 1) * ROWS]
                    size = size_of(first + u, chunk * 8 + q)
                    parts.append(coefficients(part, same, size).astype(jnp.bfloat16))
                lines.append(jnp.concatenate(parts, axis=1))
            grads = jnp.dot(
                jnp.concatenate(lines, axis=0), columns, preferred_element_type=jnp.float32
            )
            for u in range(count):
                acc[first + u] += grads[u * ROWS : (u + 1) * ROWS]

        @pl.when(distance % 4 == 0)
        def _():
            multiply(distance // 4 * 7, 1)

        @pl.when(distance % 4 != 0)
        def _():
            multiply(distance * 2 - 1, 2)

    before(group)
    for make, args in started:
        for copy in make(*args):
            copy.wait_send()


def shards(rows, labels, counts, multiplicity, scaling, offset):
    width = rows.shape[1]
    smem = pl.BlockSpec(memory_space=pltpu.SMEM)
    vmem = pl.BlockSpec(memory_space=pltpu.VMEM)
    dma = pltpu.SemaphoreType.DMA
    return pl.pallas_call(
        kernel,
        out_shape=(pltpu.VMEM if OUT_VMEM else jax.ShapeDtypeStruct)((ROWS, width), jnp.float32),
        in_specs=[smem, smem, smem, smem, vmem, vmem],
        out_specs=vmem,
        scratch_shapes=[
            pltpu.VMEM((32, ROWS, width), jnp.bfloat16),
            pltpu.VMEM((NZ, ROWS, width), jnp.bfloat16),
            pltpu.VMEM((32, 1, ROWS), jnp.int32),
            pltpu.VMEM((NZ, 1, ROWS), jnp.int32),
            pltpu.VMEM((NZ, ROWS, ROWS), jnp.float32),
            pltpu.VMEM((NZ, ROWS, width), jnp.float32),
            pltpu.VMEM((2, 4, 2, HALF, width), jnp.bfloat16),
            pltpu.VMEM((2, 4, 2, HALF, width), jnp.bfloat16),
            pltpu.SMEM((NZ,), jnp.int32),
            pltpu.SMEM((32,), jnp.int32),
            *(dma(shape) for shape in ((4, 2), (4, 4, 2), (4, 4), (NZ, 2)) for _ in range(2)),
            *(dma(shape) for shape in ((4,), (4, 4), (4, 4), (NZ,)) for _ in range(2)),
            dma((2, 4, 2)), dma((2, 4, 2)),
        ],
        compiler_params=pltpu.CompilerParams(
            collective_id=0, has_side_effects=True, vmem_limit_bytes=VMEM_MIB * 1024 * 1024
        ),
    )(multiplicity, scaling, offset, counts, rows, labels.reshape(1, ROWS))


def solution(mesh):
    return jax.shard_map(
        shards,
        mesh=mesh,
        in_specs=(
            P(("block", "piece"), None),
            P(("block", "piece")),
            P("block", "piece"),
            P(),
            P(),
            P(),
        ),
        out_specs=P(("block", "piece"), None),
        check_vma=False,
    )
```

```python
import math

import jax
import jax.numpy as jnp
from jax import lax
from jax.experimental import pallas as pl
from jax.experimental.pallas import tpu as pltpu
from jax.sharding import PartitionSpec as P

MESH = pl.DeviceIdType.MESH
ROWS = 128
HALF = 64
NX, NY, NZ = 4, 4, 8
COMPUTE = True
REDUCE = True
OUT_VMEM = True
VMEM_MIB = 60

OFFSETS = (0, 1, 3, 2)
OWN, NEXT, LAST, FAR = range(4)


def z_slot(step):
    return 2 * step - 1 if step > 0 else -2 * step


CHUNKS = (
    ((0, 0), (2, 0), (1, 0), (0, 2)),
    ((0, 1), (3, 0), (0, 3), (2, 2)),
    ((2, 1), (1, 2), (1, 1), (3, 1)),
    ((3, 2), (2, 3), (1, 3), (3, 3)),
)
ORDER = {}
for _chunk, _units in enumerate(CHUNKS):
    for _i, _unit in enumerate(_units):
        for _core in range(2):
            ORDER[(*_unit, _core)] = 8 * _chunk + 2 * _i + _core

A, B, C, Z, T, R = range(6)
PROGRAM = (
    (A, 2, 0), (A, 1, 1), (A, 2, 1), (A, 1, 0), (Z, -1, 0), (Z, 1, 1), (Z, -1, 1), (Z, 1, 0),
    (B, 0, 2, 0), (B, 0, 1, 1), (B, 0, 2, 1), (B, 0, 1, 0), (C, 0, 0), (A, 3, 0), (A, 3, 1),
    (B, 2, 2, 0), (B, 2, 1, 0), (B, 1, 1, 1), (B, 1, 2, 1), (Z, -2, 0), (Z, 2, 1), (B, 0, 3, 0),
    (B, 0, 3, 1), (B, 2, 1, 1), (B, 2, 2, 1), (B, 1, 2, 0), (B, 1, 1, 0), (C, 2, 0), (C, 1, 0),
    (Z, -2, 1), (Z, 2, 0), (C, 0, 2), (C, 0, 1), (T, 1, 0), (Z, -3, 0), (Z, 3, 1), (B, 2, 3, 0),
    (B, 3, 2, 0), (B, 3, 1, 1), (B, 3, 2, 1), (B, 3, 1, 0), (C, 3, 0), (T, 0, 0), (B, 1, 3, 1),
    (C, 0, 3), (Z, -3, 1), (Z, 3, 0), (T, 2, 0), (B, 2, 3, 1), (C, 2, 2), (C, 2, 1), (B, 1, 3, 0),
    (C, 1, 2), (C, 1, 1), (Z, 4, 0), (Z, 4, 1), (T, 2, 1), (B, 3, 3, 1), (T, 1, 1), (B, 3, 3, 0),
    (C, 3, 1), (T, 3, 0), (C, 3, 2), (T, 3, 1), (C, 2, 3), (C, 1, 3), (T, 4, 0), (C, 3, 3), (T, 4, 1),
    (T, 4, 2), (T, 4, 3), (R, 0, 0, 0), (R, 1, 0, 1), (T, 3, 2), (T, 3, 3), (R, 1, 1, 0), (R, 0, 1, 1),
    (R, 0, 1, 0), (R, 1, 1, 1), (T, 2, 2), (T, 2, 3), (R, 1, 2, 0), (R, 0, 2, 1), (T, 1, 2), (T, 1, 3),
    (R, 0, 2, 0), (R, 1, 2, 1), (T, 0, 1), (T, 0, 2), (R, 0, 3, 1), (R, 1, 3, 0), (T, 0, 3),
    (R, 1, 3, 1), (R, 0, 3, 0), (R, 1, 4, 0), (R, 0, 4, 1), (R, 1, 4, 1), (R, 0, 4, 0),
)
STEPS = tuple(entry[1:] for entry in PROGRAM if entry[0] == T)


def upward(entry):
    if entry[0] == Z:
        return entry[1] < 0 or (entry[1] == 4 and entry[2] == 0)
    return entry[-2] == LAST or (entry[-2] == FAR and entry[-1] == 0)


def needs(entry):
    kind, half = entry[0], entry[-1]
    if kind in (A, B) and entry[-2] == FAR:
        return [(*entry[:-2], NEXT if half else LAST, half)]
    if kind == B:
        return [(A, entry[1], half)] if entry[1] != OWN else []
    if kind == C:
        a, b = entry[1:]
        unit = (B, a, b) if b != OWN else (A, a)
        return [(*unit, half) for half in range(2)] if (a, b) != (OWN, OWN) else []
    if kind == Z:
        source = z_source(entry)
        return [(Z, source, half)] if source else []
    if kind == T:
        steps = [step for step in range(-3, 5) if step and abs(step) == entry[1]]
        lines = [need for unit in CHUNKS[entry[2]] for need in (*needs((C, *unit)), (C, *unit))]
        return [(Z, step, half) for step in steps for half in range(2)] + lines
    return []


def z_source(entry):
    step, half = entry[1:]
    if step == 4:
        return 3 if half else -3
    return step - 1 if step > 0 else step + 1


def carries_label(entry):
    if entry[0] == C:
        return True
    if entry[0] == Z and entry[1] != 4 or entry[0] != Z and entry[-2] != FAR:
        return entry[-1] == (0 if upward(entry) else 1)
    return entry[-1] == 0


def kernel(
    mult_in, scale_in, offset_in, count_in, x_in, lab_in, out_ref,
    mult_ref, scale_ref, offset_ref, count_ref, x_ref, input_sems,
    jbuf, ibuf, labj, labi, labcol, acc, psend, precv, row_blocks, column_blocks,
    send_a, recv_a, send_b, recv_b, send_c, recv_c, send_z, recv_z,
    lsend_a, lrecv_a, lsend_b, lrecv_b, lsend_c, lrecv_c, lsend_z, lrecv_z, send_p, recv_p,
):
    block = lax.axis_index("block")
    piece = lax.axis_index("piece")
    z = block // NY % NZ
    y = block % NY
    x = piece // 2 * 2 + block // (NY * NZ)
    c = piece % 2

    def device(px, py, pz, pc):
        return (px % 2 * (NY * NZ) + pz * NY + py, px // 2 * 2 + pc)

    def place(a, b, core):
        return (x + a * (1 - core) + b * core) % NX, (y + a * core + b * (1 - core)) % NY

    def plane_device(a, b):
        px, py = place(a, b, c)
        return device(px, py, z, c)

    other_core = device(x, y, z, 1 - c)
    a_up, a_down = plane_device(1, 0), plane_device(3, 0)
    b_up, b_down = plane_device(0, 1), plane_device(0, 3)
    z_up, z_down = device(x, y, (z + 1) % NZ, c), device(x, y, (z + NZ - 1) % NZ, c)

    def copies(entry):
        kind, half = entry[0], entry[-1]
        rows, labels, part = jbuf, labj, pl.ds(half * HALF, HALF)
        if kind in (A, B):
            unit = entry[-2]
            source = (NEXT if half else LAST) if unit == FAR else OWN
            line = (entry[1],) if kind == B else ()
            source = ORDER[(*line, source, 0)] if kind == B else ORDER[source, OWN, 0]
            target = ORDER[(*line, unit, 0)] if kind == B else ORDER[unit, OWN, 0]
            key, label_key = (*line, unit, half), (*line, unit)
            to = ((a_up, a_down), (b_up, b_down))[kind][0 if upward(entry) else 1]
            semaphores = ((send_a, recv_a, lsend_a, lrecv_a), (send_b, recv_b, lsend_b, lrecv_b))[kind]
        elif kind == C:
            a, b = entry[1:]
            source, target, part = ORDER[a, b, 0], ORDER[a, b, 1], pl.ds(0, ROWS)
            key = label_key = (a, b)
            to = other_core
            semaphores = send_c, recv_c, lsend_c, lrecv_c
        else:
            rows, labels = ibuf, labi
            source, target = z_slot(z_source(entry)), z_slot(entry[1])
            key, label_key = (target, half), (target,)
            to = z_up if upward(entry) else z_down
            semaphores = send_z, recv_z, lsend_z, lrecv_z

        def copy(source_ref, target_ref, send_sem, recv_sem):
            return pltpu.make_async_remote_copy(
                src_ref=source_ref, dst_ref=target_ref, send_sem=send_sem, recv_sem=recv_sem,
                device_id=to, device_id_type=MESH,
            )

        send, recv, lsend, lrecv = semaphores
        made = [copy(rows.at[source, part], rows.at[target, part], send.at[key], recv.at[key])]
        if carries_label(entry):
            made.append(copy(labels.at[source], labels.at[target], lsend.at[label_key], lrecv.at[label_key]))
        return made

    started = []

    def send(make, *args):
        for copy in make(*args):
            copy.start()
        started.append((make, args))

    def arrived(made):
        for copy in made:
            copy.wait_recv()

    barrier = pltpu.get_barrier_semaphore()
    for neighbour in (a_up, a_down, b_up, b_down, z_up, z_down, other_core):
        pl.semaphore_signal(barrier, inc=1, device_id=neighbour, device_id_type=MESH)

    mult_copy, scale_copy, offset_copy, count_copy, x_copy, labj_copy, labi_copy = (
        pltpu.make_async_copy(source, target, input_sems.at[i])
        for i, (source, target) in enumerate(
            (
                (mult_in, mult_ref),
                (scale_in, scale_ref),
                (offset_in, offset_ref),
                (count_in, count_ref),
                (x_in, x_ref),
                (lab_in, labj.at[0]),
                (lab_in, labi.at[0]),
            )
        )
    )
    for copy in (x_copy, count_copy, labj_copy, labi_copy, scale_copy, offset_copy, mult_copy):
        copy.start()
    count_copy.wait()
    x_copy.wait()
    live_rows = lax.broadcasted_iota(jnp.int32, (ROWS, 1), 0) // HALF < count_ref[0, 0]
    own = jnp.where(live_rows, x_ref[...], 0.0).astype(jnp.bfloat16)
    jbuf[0] = own
    ibuf[0] = own
    labj_copy.wait()
    labi_copy.wait()

    pl.semaphore_wait(barrier, 7)

    known = set()

    def take(entry):
        for need in needs(entry):
            if need not in known:
                known.add(need)
                arrived(copies(need))
        if entry[0] == R:
            pass_on(*entry[1:])
        elif entry[0] != T:
            send(copies, entry)

    first = min(i for i, entry in enumerate(PROGRAM) if needs(entry))
    for entry in PROGRAM[:first]:
        take(entry)

    for copy in (scale_copy, offset_copy, mult_copy):
        copy.wait()
    factor = 0.5 * math.sqrt(jbuf.shape[-1] / (ROWS * NX * NY * NZ * 2)) / 8.0 * scale_ref[0]
    half_scale = 0.5 * scale_ref[0]
    half_offset = 0.5 * offset_ref[0]

    for step in range(-3, 5):
        row_blocks[z_slot(step)] = x % 2 * (NY * NZ) + (z + NZ + step) % NZ * NY + y
    for (a, b, core), place_in_plane in ORDER.items():
        px, py = place(OFFSETS[a], OFFSETS[b], 1 - c if core else c)
        column_blocks[place_in_plane] = px % 2 * (NY * NZ) + z * NY + py

    def size_of(row, column):
        return factor * mult_ref[row_blocks[row], column_blocks[column]].astype(jnp.float32)

    def coefficients(scores, same, size):
        return size * jnp.tanh(half_scale * scores + half_offset) + jnp.where(same, -size, size)

    acc[...] = jnp.zeros_like(acc)
    scores = lax.dot_general(own, own, (((1,), (1,)), ((), ())), preferred_element_type=jnp.float32)
    square = (ROWS, ROWS)
    eye = lax.broadcasted_iota(jnp.int32, square, 0) == lax.broadcasted_iota(jnp.int32, square, 1)
    diagonal = jnp.where(eye, coefficients(scores, jnp.full(square, True), size_of(0, 0)), 0.0)
    acc[0] = -jnp.dot(diagonal.astype(jnp.bfloat16), own, preferred_element_type=jnp.float32)

    def partial(direction, step, half):
        return [
            pltpu.make_async_remote_copy(
                src_ref=psend.at[direction, step, half],
                dst_ref=precv.at[direction, step, half],
                send_sem=send_p.at[direction, step, half],
                recv_sem=recv_p.at[direction, step, half],
                device_id=z_down if direction else z_up,
                device_id_type=MESH,
            )
        ]

    def pass_on(direction, step, half):
        if not REDUCE:
            return
        row = z_slot(4 if step == 0 else step - 4 if direction else 4 - step)
        rows = slice(half * HALF, (half + 1) * HALF)
        value = acc[row, rows]
        if step == 4:
            if direction not in met[half]:
                arrived(partial(direction, 3, half))
                met[half].append(direction)
            if len(met[half]) == 2:
                for way in range(2):
                    value = value + precv[way, 3, half].astype(jnp.float32)
                out_ref[rows, :] = jnp.where(live_rows[rows], value, 0.0)
            return
        if step >= 2 or (step == 1 and half == direction):
            arrived(partial(direction, step - 1, half))
            value = value + precv[direction, step - 1, half].astype(jnp.float32)
        psend[direction, step, half] = value.astype(jnp.bfloat16)
        send(partial, direction, step, half)

    met = ([], [])

    def label_columns(distance):
        for i in {z_slot(distance), z_slot(-distance if distance < 4 else 4)}:
            labcol[i] = jnp.broadcast_to(labi[i].astype(jnp.float32), square).T

    groups, group, met_distances = [], [], set()
    for entry in PROGRAM[first:]:
        group.append(entry)
        if entry[0] == T:
            groups.append(group)
            group = []

    def before(entries):
        for entry in entries:
            take(entry)
            if entry[0] == T and entry[1] not in met_distances:
                met_distances.add(entry[1])
                label_columns(entry[1])

    before(groups[0])

    width = jbuf.shape[-1]

    @pl.loop(0, len(STEPS))
    def _(step):
        distance = step * 0
        chunk = step * 0
        for s, (p, k) in enumerate(STEPS):
            distance = jnp.where(step == s, p, distance)
            chunk = jnp.where(step == s, k, chunk)

            if s == 0:
                continue

            @pl.when(step == s)
            def _(s=s):
                before(groups[s])

        if not COMPUTE:
            return
        def multiply(first, count):
            columns = jbuf[pl.ds(chunk * 8, 8)].reshape(8 * ROWS, width)
            rows = ibuf[pl.ds(first, count)].reshape(count * ROWS, width)
            scores = lax.dot_general(
                rows, columns, (((1,), (1,)), ((), ())), preferred_element_type=jnp.float32
            )
            lines = []
            for u in range(count):
                parts = []
                for q in range(8):
                    same = labcol[first + u] == labj[chunk * 8 + q].astype(jnp.float32)
                    part = scores[u * ROWS : (u + 1) * ROWS, q * ROWS : (q + 1) * ROWS]
                    size = size_of(first + u, chunk * 8 + q)
                    parts.append(coefficients(part, same, size).astype(jnp.bfloat16))
                lines.append(jnp.concatenate(parts, axis=1))
            grads = jnp.dot(
                jnp.concatenate(lines, axis=0), columns, preferred_element_type=jnp.float32
            )
            for u in range(count):
                acc[first + u] += grads[u * ROWS : (u + 1) * ROWS]

        @pl.when(distance % 4 == 0)
        def _():
            multiply(distance // 4 * 7, 1)

        @pl.when(distance % 4 != 0)
        def _():
            multiply(distance * 2 - 1, 2)

    before(group)
    for make, args in started:
        for copy in make(*args):
            copy.wait_send()


def shards(rows, labels, counts, multiplicity, scaling, offset):
    width = rows.shape[1]
    hbm = pl.BlockSpec(memory_space=pltpu.HBM)
    vmem = pl.BlockSpec(memory_space=pltpu.VMEM)
    dma = pltpu.SemaphoreType.DMA
    return pl.pallas_call(
        kernel,
        out_shape=(pltpu.VMEM if OUT_VMEM else jax.ShapeDtypeStruct)((ROWS, width), jnp.float32),
        in_specs=[hbm] * 6,
        out_specs=vmem,
        scratch_shapes=[
            pltpu.SMEM(multiplicity.shape, jnp.int32),
            pltpu.SMEM((1,), jnp.float32),
            pltpu.SMEM((1,), jnp.float32),
            pltpu.SMEM((1, 1), jnp.int32),
            pltpu.VMEM((ROWS, width), jnp.float32),
            dma((7,)),
            pltpu.VMEM((32, ROWS, width), jnp.bfloat16),
            pltpu.VMEM((NZ, ROWS, width), jnp.bfloat16),
            pltpu.VMEM((32, 1, ROWS), jnp.int32),
            pltpu.VMEM((NZ, 1, ROWS), jnp.int32),
            pltpu.VMEM((NZ, ROWS, ROWS), jnp.float32),
            pltpu.VMEM((NZ, ROWS, width), jnp.float32),
            pltpu.VMEM((2, 4, 2, HALF, width), jnp.bfloat16),
            pltpu.VMEM((2, 4, 2, HALF, width), jnp.bfloat16),
            pltpu.SMEM((NZ,), jnp.int32),
            pltpu.SMEM((32,), jnp.int32),
            *(dma(shape) for shape in ((4, 2), (4, 4, 2), (4, 4), (NZ, 2)) for _ in range(2)),
            *(dma(shape) for shape in ((4,), (4, 4), (4, 4), (NZ,)) for _ in range(2)),
            dma((2, 4, 2)), dma((2, 4, 2)),
        ],
        compiler_params=pltpu.CompilerParams(
            collective_id=0, has_side_effects=True, vmem_limit_bytes=VMEM_MIB * 1024 * 1024
        ),
    )(multiplicity, scaling, offset, counts, rows, labels.reshape(1, ROWS))


def solution(mesh):
    return jax.shard_map(
        shards,
        mesh=mesh,
        in_specs=(
            P(("block", "piece"), None),
            P(("block", "piece")),
            P("block", "piece"),
            P(),
            P(),
            P(),
        ),
        out_specs=P(("block", "piece"), None),
        check_vma=False,
    )
```

```python
import math

import jax
import jax.numpy as jnp
from jax import lax
from jax.experimental import pallas as pl
from jax.experimental.pallas import tpu as pltpu
from jax.sharding import PartitionSpec as P

MESH = pl.DeviceIdType.MESH
ROWS = 128
HALF = 64
NX, NY, NZ = 4, 4, 8
COMPUTE = True
REDUCE = True
OUT_VMEM = True
VMEM_MIB = 60

OFFSETS = (0, 1, 3, 2)
OWN, NEXT, LAST, FAR = range(4)


def z_slot(step):
    return 2 * step - 1 if step > 0 else -2 * step


CHUNKS = (
    ((0, 0), (2, 0), (1, 0), (0, 2)),
    ((0, 1), (3, 0), (0, 3), (2, 2)),
    ((2, 1), (1, 2), (1, 1), (3, 1)),
    ((3, 2), (2, 3), (1, 3), (3, 3)),
)
ORDER = {}
for _chunk, _units in enumerate(CHUNKS):
    for _i, _unit in enumerate(_units):
        for _core in range(2):
            ORDER[(*_unit, _core)] = 8 * _chunk + 2 * _i + _core

A, B, C, Z, T, R = range(6)
PROGRAM = (
    (A, 2, 0), (A, 1, 1), (A, 2, 1), (A, 1, 0), (Z, -1, 0), (Z, 1, 1), (Z, -1, 1), (Z, 1, 0),
    (B, 0, 2, 0), (B, 0, 1, 1), (B, 0, 2, 1), (B, 0, 1, 0), (C, 0, 0), (A, 3, 0), (A, 3, 1),
    (B, 2, 2, 0), (B, 2, 1, 0), (B, 1, 1, 1), (B, 1, 2, 1), (Z, -2, 0), (Z, 2, 1), (B, 0, 3, 0),
    (B, 0, 3, 1), (B, 2, 1, 1), (B, 2, 2, 1), (B, 1, 2, 0), (B, 1, 1, 0), (C, 2, 0), (C, 1, 0),
    (Z, -2, 1), (Z, 2, 0), (C, 0, 2), (C, 0, 1), (T, 1, 0), (Z, -3, 0), (Z, 3, 1), (B, 2, 3, 0),
    (B, 3, 2, 0), (B, 3, 1, 1), (B, 3, 2, 1), (B, 3, 1, 0), (C, 3, 0), (T, 0, 0), (B, 1, 3, 1),
    (C, 0, 3), (Z, -3, 1), (Z, 3, 0), (T, 2, 0), (B, 2, 3, 1), (C, 2, 2), (C, 2, 1), (B, 1, 3, 0),
    (C, 1, 2), (C, 1, 1), (Z, 4, 0), (Z, 4, 1), (T, 2, 1), (B, 3, 3, 1), (T, 1, 1), (B, 3, 3, 0),
    (C, 3, 1), (T, 3, 0), (C, 3, 2), (T, 3, 1), (C, 2, 3), (C, 1, 3), (T, 4, 0), (C, 3, 3), (T, 4, 1),
    (T, 4, 2), (T, 4, 3), (R, 0, 0, 0), (R, 1, 0, 1), (T, 3, 2), (T, 3, 3), (R, 1, 1, 0), (R, 0, 1, 1),
    (R, 0, 1, 0), (R, 1, 1, 1), (T, 2, 2), (T, 2, 3), (R, 1, 2, 0), (R, 0, 2, 1), (T, 1, 2), (T, 1, 3),
    (R, 0, 2, 0), (R, 1, 2, 1), (T, 0, 1), (T, 0, 2), (R, 0, 3, 1), (R, 1, 3, 0), (T, 0, 3),
    (R, 1, 3, 1), (R, 0, 3, 0), (R, 1, 4, 0), (R, 0, 4, 1), (R, 1, 4, 1), (R, 0, 4, 0),
)
STEPS = tuple(entry[1:] for entry in PROGRAM if entry[0] == T)


def upward(entry):
    if entry[0] == Z:
        return entry[1] < 0 or (entry[1] == 4 and entry[2] == 0)
    return entry[-2] == LAST or (entry[-2] == FAR and entry[-1] == 0)


def needs(entry):
    kind, half = entry[0], entry[-1]
    if kind in (A, B) and entry[-2] == FAR:
        return [(*entry[:-2], NEXT if half else LAST, half)]
    if kind == B:
        return [(A, entry[1], half)] if entry[1] != OWN else []
    if kind == C:
        a, b = entry[1:]
        unit = (B, a, b) if b != OWN else (A, a)
        return [(*unit, half) for half in range(2)] if (a, b) != (OWN, OWN) else []
    if kind == Z:
        source = z_source(entry)
        return [(Z, source, half)] if source else []
    if kind == T:
        steps = [step for step in range(-3, 5) if step and abs(step) == entry[1]]
        lines = [need for unit in CHUNKS[entry[2]] for need in (*needs((C, *unit)), (C, *unit))]
        return [(Z, step, half) for step in steps for half in range(2)] + lines
    return []


def z_source(entry):
    step, half = entry[1:]
    if step == 4:
        return 3 if half else -3
    return step - 1 if step > 0 else step + 1


def carries_label(entry):
    if entry[0] == C:
        return True
    if entry[0] == Z and entry[1] != 4 or entry[0] != Z and entry[-2] != FAR:
        return entry[-1] == (0 if upward(entry) else 1)
    return entry[-1] == 0


def kernel(
    mult_in, scale_in, offset_in, count_in, x_in, lab_in, out_ref,
    mult_ref, scale_ref, offset_ref, count_ref, x_ref, input_sems,
    jbuf, ibuf, labj, labi, labcol, acc, psend, precv, row_blocks, column_blocks,
    send_a, recv_a, send_b, recv_b, send_c, recv_c, send_z, recv_z,
    lsend_a, lrecv_a, lsend_b, lrecv_b, lsend_c, lrecv_c, lsend_z, lrecv_z, send_p, recv_p,
):
    block = lax.axis_index("block")
    piece = lax.axis_index("piece")
    z = block // NY % NZ
    y = block % NY
    x = piece // 2 * 2 + block // (NY * NZ)
    c = piece % 2

    def device(px, py, pz, pc):
        return (px % 2 * (NY * NZ) + pz * NY + py, px // 2 * 2 + pc)

    def place(a, b, core):
        return (x + a * (1 - core) + b * core) % NX, (y + a * core + b * (1 - core)) % NY

    def plane_device(a, b):
        px, py = place(a, b, c)
        return device(px, py, z, c)

    other_core = device(x, y, z, 1 - c)
    a_up, a_down = plane_device(1, 0), plane_device(3, 0)
    b_up, b_down = plane_device(0, 1), plane_device(0, 3)
    z_up, z_down = device(x, y, (z + 1) % NZ, c), device(x, y, (z + NZ - 1) % NZ, c)

    def copies(entry):
        kind, half = entry[0], entry[-1]
        rows, labels, part = jbuf, labj, pl.ds(half * HALF, HALF)
        if kind in (A, B):
            unit = entry[-2]
            source = (NEXT if half else LAST) if unit == FAR else OWN
            line = (entry[1],) if kind == B else ()
            source = ORDER[(*line, source, 0)] if kind == B else ORDER[source, OWN, 0]
            target = ORDER[(*line, unit, 0)] if kind == B else ORDER[unit, OWN, 0]
            key, label_key = (*line, unit, half), (*line, unit)
            to = ((a_up, a_down), (b_up, b_down))[kind][0 if upward(entry) else 1]
            semaphores = ((send_a, recv_a, lsend_a, lrecv_a), (send_b, recv_b, lsend_b, lrecv_b))[kind]
        elif kind == C:
            a, b = entry[1:]
            source, target, part = ORDER[a, b, 0], ORDER[a, b, 1], pl.ds(0, ROWS)
            key = label_key = (a, b)
            to = other_core
            semaphores = send_c, recv_c, lsend_c, lrecv_c
        else:
            rows, labels = ibuf, labi
            source, target = z_slot(z_source(entry)), z_slot(entry[1])
            key, label_key = (target, half), (target,)
            to = z_up if upward(entry) else z_down
            semaphores = send_z, recv_z, lsend_z, lrecv_z

        def copy(source_ref, target_ref, send_sem, recv_sem):
            return pltpu.make_async_remote_copy(
                src_ref=source_ref, dst_ref=target_ref, send_sem=send_sem, recv_sem=recv_sem,
                device_id=to, device_id_type=MESH,
            )

        send, recv, lsend, lrecv = semaphores
        made = [copy(rows.at[source, part], rows.at[target, part], send.at[key], recv.at[key])]
        if carries_label(entry):
            made.append(copy(labels.at[source], labels.at[target], lsend.at[label_key], lrecv.at[label_key]))
        return made

    started = []

    def send(make, *args):
        for copy in make(*args):
            copy.start()
        started.append((make, args))

    def arrived(made):
        for copy in made:
            copy.wait_recv()

    barrier = pltpu.get_barrier_semaphore()
    for neighbour in (a_up, a_down, b_up, b_down, z_up, z_down, other_core):
        pl.semaphore_signal(barrier, inc=1, device_id=neighbour, device_id_type=MESH)

    mult_copy, scale_copy, offset_copy, count_copy, x_copy, labj_copy, labi_copy = (
        pltpu.make_async_copy(source, target, input_sems.at[i])
        for i, (source, target) in enumerate(
            (
                (mult_in, mult_ref),
                (scale_in, scale_ref),
                (offset_in, offset_ref),
                (count_in, count_ref),
                (x_in, x_ref),
                (lab_in, labj.at[0]),
                (lab_in, labi.at[0]),
            )
        )
    )
    for copy in (x_copy, count_copy, labj_copy, labi_copy, scale_copy, offset_copy, mult_copy):
        copy.start()
    count_copy.wait()
    x_copy.wait()
    live_rows = lax.broadcasted_iota(jnp.int32, (ROWS, 1), 0) // HALF < count_ref[0, 0]
    own = jnp.where(live_rows, x_ref[...], 0.0).astype(jnp.bfloat16)
    jbuf[0] = own
    ibuf[0] = own
    labj_copy.wait()
    labi_copy.wait()

    pl.semaphore_wait(barrier, 7)

    known = set()

    def take(entry):
        for need in needs(entry):
            if need not in known:
                known.add(need)
                arrived(copies(need))
        if entry[0] == R:
            pass_on(*entry[1:])
        elif entry[0] != T:
            send(copies, entry)

    first = min(i for i, entry in enumerate(PROGRAM) if needs(entry))
    for entry in PROGRAM[:first]:
        take(entry)

    for copy in (scale_copy, offset_copy, mult_copy):
        copy.wait()
    factor = math.sqrt(jbuf.shape[-1] / (ROWS * NX * NY * NZ * 2)) / 8.0 * scale_ref[0]
    scale = scale_ref[0]
    offset = offset_ref[0]

    for step in range(-3, 5):
        row_blocks[z_slot(step)] = x % 2 * (NY * NZ) + (z + NZ + step) % NZ * NY + y
    for (a, b, core), place_in_plane in ORDER.items():
        px, py = place(OFFSETS[a], OFFSETS[b], 1 - c if core else c)
        column_blocks[place_in_plane] = px % 2 * (NY * NZ) + z * NY + py

    def size_of(row, column):
        return factor * mult_ref[row_blocks[row], column_blocks[column]].astype(jnp.float32)

    def coefficients(scores, same, size):
        logits = scale * scores + offset
        return jnp.where(same, -size, size) / (1.0 + jnp.exp(jnp.where(same, logits, -logits)))

    acc[...] = jnp.zeros_like(acc)
    scores = lax.dot_general(own, own, (((1,), (1,)), ((), ())), preferred_element_type=jnp.float32)
    square = (ROWS, ROWS)
    eye = lax.broadcasted_iota(jnp.int32, square, 0) == lax.broadcasted_iota(jnp.int32, square, 1)
    diagonal = jnp.where(eye, coefficients(scores, jnp.full(square, True), size_of(0, 0)), 0.0)
    acc[0] = -jnp.dot(diagonal.astype(jnp.bfloat16), own, preferred_element_type=jnp.float32)

    def partial(direction, step, half):
        return [
            pltpu.make_async_remote_copy(
                src_ref=psend.at[direction, step, half],
                dst_ref=precv.at[direction, step, half],
                send_sem=send_p.at[direction, step, half],
                recv_sem=recv_p.at[direction, step, half],
                device_id=z_down if direction else z_up,
                device_id_type=MESH,
            )
        ]

    def pass_on(direction, step, half):
        if not REDUCE:
            return
        row = z_slot(4 if step == 0 else step - 4 if direction else 4 - step)
        rows = slice(half * HALF, (half + 1) * HALF)
        value = acc[row, rows]
        if step == 4:
            if direction not in met[half]:
                arrived(partial(direction, 3, half))
                met[half].append(direction)
            if len(met[half]) == 2:
                for way in range(2):
                    value = value + precv[way, 3, half].astype(jnp.float32)
                out_ref[rows, :] = jnp.where(live_rows[rows], value, 0.0)
            return
        if step >= 2 or (step == 1 and half == direction):
            arrived(partial(direction, step - 1, half))
            value = value + precv[direction, step - 1, half].astype(jnp.float32)
        psend[direction, step, half] = value.astype(jnp.bfloat16)
        send(partial, direction, step, half)

    met = ([], [])

    def label_columns(distance):
        for i in {z_slot(distance), z_slot(-distance if distance < 4 else 4)}:
            labcol[i] = jnp.broadcast_to(labi[i].astype(jnp.float32), square).T

    groups, group, met_distances = [], [], set()
    for entry in PROGRAM[first:]:
        group.append(entry)
        if entry[0] == T:
            groups.append(group)
            group = []

    def before(entries):
        for entry in entries:
            take(entry)
            if entry[0] == T and entry[1] not in met_distances:
                met_distances.add(entry[1])
                label_columns(entry[1])

    before(groups[0])

    width = jbuf.shape[-1]

    @pl.loop(0, len(STEPS))
    def _(step):
        distance = step * 0
        chunk = step * 0
        for s, (p, k) in enumerate(STEPS):
            distance = jnp.where(step == s, p, distance)
            chunk = jnp.where(step == s, k, chunk)

            if s == 0:
                continue

            @pl.when(step == s)
            def _(s=s):
                before(groups[s])

        if not COMPUTE:
            return
        def multiply(first, count):
            columns = jbuf[pl.ds(chunk * 8, 8)].reshape(8 * ROWS, width)
            rows = ibuf[pl.ds(first, count)].reshape(count * ROWS, width)
            scores = lax.dot_general(
                rows, columns, (((1,), (1,)), ((), ())), preferred_element_type=jnp.float32
            )
            lines = []
            for u in range(count):
                parts = []
                for q in range(8):
                    same = labcol[first + u] == labj[chunk * 8 + q].astype(jnp.float32)
                    part = scores[u * ROWS : (u + 1) * ROWS, q * ROWS : (q + 1) * ROWS]
                    size = size_of(first + u, chunk * 8 + q)
                    parts.append(coefficients(part, same, size).astype(jnp.bfloat16))
                lines.append(jnp.concatenate(parts, axis=1))
            grads = jnp.dot(
                jnp.concatenate(lines, axis=0), columns, preferred_element_type=jnp.float32
            )
            for u in range(count):
                acc[first + u] += grads[u * ROWS : (u + 1) * ROWS]

        @pl.when(distance % 4 == 0)
        def _():
            multiply(distance // 4 * 7, 1)

        @pl.when(distance % 4 != 0)
        def _():
            multiply(distance * 2 - 1, 2)

    before(group)
    for make, args in started:
        for copy in make(*args):
            copy.wait_send()


def shards(rows, labels, counts, multiplicity, scaling, offset):
    width = rows.shape[1]
    hbm = pl.BlockSpec(memory_space=pltpu.HBM)
    vmem = pl.BlockSpec(memory_space=pltpu.VMEM)
    dma = pltpu.SemaphoreType.DMA
    return pl.pallas_call(
        kernel,
        out_shape=(pltpu.VMEM if OUT_VMEM else jax.ShapeDtypeStruct)((ROWS, width), jnp.float32),
        in_specs=[hbm] * 6,
        out_specs=vmem,
        scratch_shapes=[
            pltpu.SMEM(multiplicity.shape, jnp.int32),
            pltpu.SMEM((1,), jnp.float32),
            pltpu.SMEM((1,), jnp.float32),
            pltpu.SMEM((1, 1), jnp.int32),
            pltpu.VMEM((ROWS, width), jnp.float32),
            dma((7,)),
            pltpu.VMEM((32, ROWS, width), jnp.bfloat16),
            pltpu.VMEM((NZ, ROWS, width), jnp.bfloat16),
            pltpu.VMEM((32, 1, ROWS), jnp.int32),
            pltpu.VMEM((NZ, 1, ROWS), jnp.int32),
            pltpu.VMEM((NZ, ROWS, ROWS), jnp.float32),
            pltpu.VMEM((NZ, ROWS, width), jnp.float32),
            pltpu.VMEM((2, 4, 2, HALF, width), jnp.bfloat16),
            pltpu.VMEM((2, 4, 2, HALF, width), jnp.bfloat16),
            pltpu.SMEM((NZ,), jnp.int32),
            pltpu.SMEM((32,), jnp.int32),
            *(dma(shape) for shape in ((4, 2), (4, 4, 2), (4, 4), (NZ, 2)) for _ in range(2)),
            *(dma(shape) for shape in ((4,), (4, 4), (4, 4), (NZ,)) for _ in range(2)),
            dma((2, 4, 2)), dma((2, 4, 2)),
        ],
        compiler_params=pltpu.CompilerParams(
            collective_id=0, has_side_effects=True, vmem_limit_bytes=VMEM_MIB * 1024 * 1024
        ),
    )(multiplicity, scaling, offset, counts, rows, labels.reshape(1, ROWS))


def solution(mesh):
    return jax.shard_map(
        shards,
        mesh=mesh,
        in_specs=(
            P(("block", "piece"), None),
            P(("block", "piece")),
            P("block", "piece"),
            P(),
            P(),
            P(),
        ),
        out_specs=P(("block", "piece"), None),
        check_vma=False,
    )
```

```python
import math

import jax
import jax.numpy as jnp
from jax import lax
from jax.experimental import pallas as pl
from jax.experimental.pallas import tpu as pltpu
from jax.sharding import PartitionSpec as P

MESH = pl.DeviceIdType.MESH
ROWS = 128
HALF = 64
NX, NY, NZ = 4, 4, 8
COMPUTE = True
REDUCE = True
OUT_VMEM = True
VMEM_MIB = 60

OFFSETS = (0, 1, 3, 2)
OWN, NEXT, LAST, FAR = range(4)


def z_slot(step):
    return 2 * step - 1 if step > 0 else -2 * step


CHUNKS = (
    ((0, 0), (2, 0), (1, 0), (3, 0)),
    ((0, 2), (0, 1), (2, 2), (2, 1)),
    ((1, 2), (1, 1), (0, 3), (3, 2)),
    ((3, 1), (2, 3), (1, 3), (3, 3)),
)
ORDER = {}
for _chunk, _units in enumerate(CHUNKS):
    for _i, _unit in enumerate(_units):
        for _core in range(2):
            ORDER[(*_unit, _core)] = 8 * _chunk + 2 * _i + _core

A, B, C, Z, T, R = range(6)
PROGRAM = (
    (A, 2, 0), (A, 1, 1), (A, 2, 1), (A, 1, 0), (Z, -1, 0), (Z, 1, 1), (Z, -1, 1), (Z, 1, 0),
    (C, 0, 0), (A, 3, 0), (A, 3, 1), (B, 0, 2, 0), (B, 0, 1, 1), (B, 0, 2, 1), (B, 0, 1, 0),
    (B, 2, 2, 0), (B, 2, 1, 0), (B, 1, 1, 1), (B, 1, 2, 1), (B, 2, 1, 1), (B, 2, 2, 1), (B, 1, 2, 0),
    (B, 1, 1, 0), (Z, -2, 0), (Z, 2, 1), (C, 2, 0), (C, 1, 0), (B, 3, 2, 0), (B, 0, 3, 0),
    (B, 0, 3, 1), (B, 3, 1, 1), (B, 3, 2, 1), (Z, -2, 1), (Z, 2, 0), (B, 3, 1, 0), (C, 3, 0),
    (T, 1, 0), (Z, -3, 0), (Z, 3, 1), (B, 2, 3, 0), (C, 0, 2), (C, 0, 1), (T, 0, 0), (B, 1, 3, 1),
    (C, 2, 2), (B, 2, 3, 1), (C, 2, 1), (Z, -3, 1), (Z, 3, 0), (T, 2, 0), (B, 1, 3, 0), (C, 1, 2),
    (C, 1, 1), (T, 2, 1), (Z, 4, 0), (Z, 4, 1), (B, 3, 3, 0), (T, 1, 1), (B, 3, 3, 1), (C, 0, 3),
    (T, 0, 1), (C, 3, 2), (C, 3, 1), (T, 3, 0), (T, 3, 1), (C, 2, 3), (C, 1, 3), (T, 4, 0), (C, 3, 3),
    (T, 4, 1), (T, 4, 2), (T, 4, 3), (R, 0, 0, 0), (R, 1, 0, 1), (T, 3, 2), (T, 3, 3), (R, 1, 1, 0),
    (R, 0, 1, 1), (R, 0, 1, 0), (R, 1, 1, 1), (T, 2, 2), (T, 2, 3), (R, 0, 2, 1), (R, 1, 2, 0),
    (T, 1, 2), (T, 1, 3), (R, 0, 2, 0), (R, 1, 2, 1), (T, 0, 2), (T, 0, 3), (R, 0, 3, 1), (R, 1, 3, 0),
    (R, 1, 3, 1), (R, 0, 3, 0), (R, 1, 4, 0), (R, 0, 4, 1), (R, 1, 4, 1), (R, 0, 4, 0),
)
STEPS = tuple(entry[1:] for entry in PROGRAM if entry[0] == T)


def upward(entry):
    if entry[0] == Z:
        return entry[1] < 0 or (entry[1] == 4 and entry[2] == 0)
    return entry[-2] == LAST or (entry[-2] == FAR and entry[-1] == 0)


def needs(entry):
    kind, half = entry[0], entry[-1]
    if kind in (A, B) and entry[-2] == FAR:
        return [(*entry[:-2], NEXT if half else LAST, half)]
    if kind == B:
        return [(A, entry[1], half)] if entry[1] != OWN else []
    if kind == C:
        a, b = entry[1:]
        unit = (B, a, b) if b != OWN else (A, a)
        return [(*unit, half) for half in range(2)] if (a, b) != (OWN, OWN) else []
    if kind == Z:
        source = z_source(entry)
        return [(Z, source, half)] if source else []
    if kind == T:
        steps = [step for step in range(-3, 5) if step and abs(step) == entry[1]]
        lines = [need for unit in CHUNKS[entry[2]] for need in (*needs((C, *unit)), (C, *unit))]
        return [(Z, step, half) for step in steps for half in range(2)] + lines
    return []


def z_source(entry):
    step, half = entry[1:]
    if step == 4:
        return 3 if half else -3
    return step - 1 if step > 0 else step + 1


def carries_label(entry):
    if entry[0] == C:
        return True
    if entry[0] == Z and entry[1] != 4 or entry[0] != Z and entry[-2] != FAR:
        return entry[-1] == (0 if upward(entry) else 1)
    return entry[-1] == 0


def kernel(
    mult_in, scale_in, offset_in, count_in, x_in, lab_in, out_ref,
    mult_ref, scale_ref, offset_ref, count_ref, x_ref, input_sems,
    jbuf, ibuf, labj, labi, labcol, acc, psend, precv, row_blocks, column_blocks,
    send_a, recv_a, send_b, recv_b, send_c, recv_c, send_z, recv_z,
    lsend_a, lrecv_a, lsend_b, lrecv_b, lsend_c, lrecv_c, lsend_z, lrecv_z, send_p, recv_p,
):
    block = lax.axis_index("block")
    piece = lax.axis_index("piece")
    z = block // NY % NZ
    y = block % NY
    x = piece // 2 * 2 + block // (NY * NZ)
    c = piece % 2

    def device(px, py, pz, pc):
        return (px % 2 * (NY * NZ) + pz * NY + py, px // 2 * 2 + pc)

    def place(a, b, core):
        return (x + a * (1 - core) + b * core) % NX, (y + a * core + b * (1 - core)) % NY

    def plane_device(a, b):
        px, py = place(a, b, c)
        return device(px, py, z, c)

    other_core = device(x, y, z, 1 - c)
    a_up, a_down = plane_device(1, 0), plane_device(3, 0)
    b_up, b_down = plane_device(0, 1), plane_device(0, 3)
    z_up, z_down = device(x, y, (z + 1) % NZ, c), device(x, y, (z + NZ - 1) % NZ, c)

    def copies(entry):
        kind, half = entry[0], entry[-1]
        rows, labels, part = jbuf, labj, pl.ds(half * HALF, HALF)
        if kind in (A, B):
            unit = entry[-2]
            source = (NEXT if half else LAST) if unit == FAR else OWN
            line = (entry[1],) if kind == B else ()
            source = ORDER[(*line, source, 0)] if kind == B else ORDER[source, OWN, 0]
            target = ORDER[(*line, unit, 0)] if kind == B else ORDER[unit, OWN, 0]
            key, label_key = (*line, unit, half), (*line, unit)
            to = ((a_up, a_down), (b_up, b_down))[kind][0 if upward(entry) else 1]
            semaphores = ((send_a, recv_a, lsend_a, lrecv_a), (send_b, recv_b, lsend_b, lrecv_b))[kind]
        elif kind == C:
            a, b = entry[1:]
            source, target, part = ORDER[a, b, 0], ORDER[a, b, 1], pl.ds(0, ROWS)
            key = label_key = (a, b)
            to = other_core
            semaphores = send_c, recv_c, lsend_c, lrecv_c
        else:
            rows, labels = ibuf, labi
            source, target = z_slot(z_source(entry)), z_slot(entry[1])
            key, label_key = (target, half), (target,)
            to = z_up if upward(entry) else z_down
            semaphores = send_z, recv_z, lsend_z, lrecv_z

        def copy(source_ref, target_ref, send_sem, recv_sem):
            return pltpu.make_async_remote_copy(
                src_ref=source_ref, dst_ref=target_ref, send_sem=send_sem, recv_sem=recv_sem,
                device_id=to, device_id_type=MESH,
            )

        send, recv, lsend, lrecv = semaphores
        made = [copy(rows.at[source, part], rows.at[target, part], send.at[key], recv.at[key])]
        if carries_label(entry):
            made.append(copy(labels.at[source], labels.at[target], lsend.at[label_key], lrecv.at[label_key]))
        return made

    started = []

    def send(make, *args):
        for copy in make(*args):
            copy.start()
        started.append((make, args))

    def arrived(made):
        for copy in made:
            copy.wait_recv()

    barrier = pltpu.get_barrier_semaphore()
    for neighbour in (a_up, a_down, b_up, b_down, z_up, z_down, other_core):
        pl.semaphore_signal(barrier, inc=1, device_id=neighbour, device_id_type=MESH)

    mult_copy, scale_copy, offset_copy, count_copy, x_copy, labj_copy, labi_copy = (
        pltpu.make_async_copy(source, target, input_sems.at[i])
        for i, (source, target) in enumerate(
            (
                (mult_in, mult_ref),
                (scale_in, scale_ref),
                (offset_in, offset_ref),
                (count_in, count_ref),
                (x_in, x_ref),
                (lab_in, labj.at[0]),
                (lab_in, labi.at[0]),
            )
        )
    )
    for copy in (x_copy, count_copy, labj_copy, labi_copy, scale_copy, offset_copy, mult_copy):
        copy.start()
    count_copy.wait()
    x_copy.wait()
    live_rows = lax.broadcasted_iota(jnp.int32, (ROWS, 1), 0) // HALF < count_ref[0, 0]
    own = jnp.where(live_rows, x_ref[...], 0.0).astype(jnp.bfloat16)
    jbuf[0] = own
    ibuf[0] = own
    labj_copy.wait()
    labi_copy.wait()

    pl.semaphore_wait(barrier, 7)

    known = set()

    def take(entry):
        for need in needs(entry):
            if need not in known:
                known.add(need)
                arrived(copies(need))
        if entry[0] == R:
            pass_on(*entry[1:])
        elif entry[0] != T:
            send(copies, entry)

    first = min(i for i, entry in enumerate(PROGRAM) if needs(entry))
    for entry in PROGRAM[:first]:
        take(entry)

    for copy in (scale_copy, offset_copy, mult_copy):
        copy.wait()
    factor = math.sqrt(jbuf.shape[-1] / (ROWS * NX * NY * NZ * 2)) / 8.0 * scale_ref[0]
    scale = scale_ref[0]
    offset = offset_ref[0]

    for step in range(-3, 5):
        row_blocks[z_slot(step)] = x % 2 * (NY * NZ) + (z + NZ + step) % NZ * NY + y
    for (a, b, core), place_in_plane in ORDER.items():
        px, py = place(OFFSETS[a], OFFSETS[b], 1 - c if core else c)
        column_blocks[place_in_plane] = px % 2 * (NY * NZ) + z * NY + py

    def size_of(row, column):
        return factor * mult_ref[row_blocks[row], column_blocks[column]].astype(jnp.float32)

    def coefficients(scores, same, size):
        logits = scale * scores + offset
        return jnp.where(same, -size, size) / (1.0 + jnp.exp(jnp.where(same, logits, -logits)))

    acc[...] = jnp.zeros_like(acc)
    scores = lax.dot_general(own, own, (((1,), (1,)), ((), ())), preferred_element_type=jnp.float32)
    square = (ROWS, ROWS)
    eye = lax.broadcasted_iota(jnp.int32, square, 0) == lax.broadcasted_iota(jnp.int32, square, 1)
    diagonal = jnp.where(eye, coefficients(scores, jnp.full(square, True), size_of(0, 0)), 0.0)
    acc[0] = -jnp.dot(diagonal.astype(jnp.bfloat16), own, preferred_element_type=jnp.float32)

    def partial(direction, step, half):
        return [
            pltpu.make_async_remote_copy(
                src_ref=psend.at[direction, step, half],
                dst_ref=precv.at[direction, step, half],
                send_sem=send_p.at[direction, step, half],
                recv_sem=recv_p.at[direction, step, half],
                device_id=z_down if direction else z_up,
                device_id_type=MESH,
            )
        ]

    def pass_on(direction, step, half):
        if not REDUCE:
            return
        row = z_slot(4 if step == 0 else step - 4 if direction else 4 - step)
        rows = slice(half * HALF, (half + 1) * HALF)
        value = acc[row, rows]
        if step == 4:
            if direction not in met[half]:
                arrived(partial(direction, 3, half))
                met[half].append(direction)
            if len(met[half]) == 2:
                for way in range(2):
                    value = value + precv[way, 3, half].astype(jnp.float32)
                out_ref[rows, :] = jnp.where(live_rows[rows], value, 0.0)
            return
        if step >= 2 or (step == 1 and half == direction):
            arrived(partial(direction, step - 1, half))
            value = value + precv[direction, step - 1, half].astype(jnp.float32)
        psend[direction, step, half] = value.astype(jnp.bfloat16)
        send(partial, direction, step, half)

    met = ([], [])

    def label_columns(distance):
        for i in {z_slot(distance), z_slot(-distance if distance < 4 else 4)}:
            labcol[i] = jnp.broadcast_to(labi[i].astype(jnp.float32), square).T

    groups, group, met_distances = [], [], set()
    for entry in PROGRAM[first:]:
        group.append(entry)
        if entry[0] == T:
            groups.append(group)
            group = []

    def before(entries):
        for entry in entries:
            take(entry)
            if entry[0] == T and entry[1] not in met_distances:
                met_distances.add(entry[1])
                label_columns(entry[1])

    before(groups[0])

    width = jbuf.shape[-1]

    @pl.loop(0, len(STEPS))
    def _(step):
        distance = step * 0
        chunk = step * 0
        for s, (p, k) in enumerate(STEPS):
            distance = jnp.where(step == s, p, distance)
            chunk = jnp.where(step == s, k, chunk)

            if s == 0:
                continue

            @pl.when(step == s)
            def _(s=s):
                before(groups[s])

        if not COMPUTE:
            return
        def multiply(first, count):
            columns = jbuf[pl.ds(chunk * 8, 8)].reshape(8 * ROWS, width)
            rows = ibuf[pl.ds(first, count)].reshape(count * ROWS, width)
            scores = lax.dot_general(
                rows, columns, (((1,), (1,)), ((), ())), preferred_element_type=jnp.float32
            )
            lines = []
            for u in range(count):
                parts = []
                for q in range(8):
                    same = labcol[first + u] == labj[chunk * 8 + q].astype(jnp.float32)
                    part = scores[u * ROWS : (u + 1) * ROWS, q * ROWS : (q + 1) * ROWS]
                    size = size_of(first + u, chunk * 8 + q)
                    parts.append(coefficients(part, same, size).astype(jnp.bfloat16))
                lines.append(jnp.concatenate(parts, axis=1))
            grads = jnp.dot(
                jnp.concatenate(lines, axis=0), columns, preferred_element_type=jnp.float32
            )
            for u in range(count):
                acc[first + u] += grads[u * ROWS : (u + 1) * ROWS]

        @pl.when(distance % 4 == 0)
        def _():
            multiply(distance // 4 * 7, 1)

        @pl.when(distance % 4 != 0)
        def _():
            multiply(distance * 2 - 1, 2)

    before(group)
    for make, args in started:
        for copy in make(*args):
            copy.wait_send()


def shards(rows, labels, counts, multiplicity, scaling, offset):
    width = rows.shape[1]
    hbm = pl.BlockSpec(memory_space=pltpu.HBM)
    vmem = pl.BlockSpec(memory_space=pltpu.VMEM)
    dma = pltpu.SemaphoreType.DMA
    return pl.pallas_call(
        kernel,
        out_shape=(pltpu.VMEM if OUT_VMEM else jax.ShapeDtypeStruct)((ROWS, width), jnp.float32),
        in_specs=[hbm] * 6,
        out_specs=vmem,
        scratch_shapes=[
            pltpu.SMEM(multiplicity.shape, jnp.int32),
            pltpu.SMEM((1,), jnp.float32),
            pltpu.SMEM((1,), jnp.float32),
            pltpu.SMEM((1, 1), jnp.int32),
            pltpu.VMEM((ROWS, width), jnp.float32),
            dma((7,)),
            pltpu.VMEM((32, ROWS, width), jnp.bfloat16),
            pltpu.VMEM((NZ, ROWS, width), jnp.bfloat16),
            pltpu.VMEM((32, 1, ROWS), jnp.int32),
            pltpu.VMEM((NZ, 1, ROWS), jnp.int32),
            pltpu.VMEM((NZ, ROWS, ROWS), jnp.float32),
            pltpu.VMEM((NZ, ROWS, width), jnp.float32),
            pltpu.VMEM((2, 4, 2, HALF, width), jnp.bfloat16),
            pltpu.VMEM((2, 4, 2, HALF, width), jnp.bfloat16),
            pltpu.SMEM((NZ,), jnp.int32),
            pltpu.SMEM((32,), jnp.int32),
            *(dma(shape) for shape in ((4, 2), (4, 4, 2), (4, 4), (NZ, 2)) for _ in range(2)),
            *(dma(shape) for shape in ((4,), (4, 4), (4, 4), (NZ,)) for _ in range(2)),
            dma((2, 4, 2)), dma((2, 4, 2)),
        ],
        compiler_params=pltpu.CompilerParams(
            collective_id=0, has_side_effects=True, vmem_limit_bytes=VMEM_MIB * 1024 * 1024
        ),
    )(multiplicity, scaling, offset, counts, rows, labels.reshape(1, ROWS))


def solution(mesh):
    return jax.shard_map(
        shards,
        mesh=mesh,
        in_specs=(
            P(("block", "piece"), None),
            P(("block", "piece")),
            P("block", "piece"),
            P(),
            P(),
            P(),
        ),
        out_specs=P(("block", "piece"), None),
        check_vma=False,
    )
```
